128 devices in a mesh: row: 8 (over x_hi, z), col: 16 (over x_lo, y, core).
Axes of the slice: x: 4 (x_hi: 2, x_lo: 2; x = x_hi * 2 + x_lo), y: 4, z: 4, core: 2. Of those that a mesh axis runs over, the one named last changes fastest.
Arguments:
- latent: float32 [2, 2048, 4096], P(None, 'row', 'col'), may hold values from -3 to 3
- momentum: float32 [2, 2048, 4096], P(None, 'row', 'col'), may hold values from -4 to 4
- hyper_params: float32 [2, 2], replicated, may hold values from 0.3 to 0.7
- velocity: float32 [2, 2], replicated, may hold values from -3 to 3
- step_size: float32 [2], replicated, may hold values from 0.08 to 0.12
- counts: int32 [2048, 4096], P('row', 'col'), may hold values from 0 to 7
- kappa_field: float32 [2048, 4096], P('row', 'col'), may hold values from 0.1 to 1
Outputs:
- latent_out: float32 [2, 2048, 4096], P(None, 'row', 'col')
- momentum_out: float32 [2, 2048, 4096], P(None, 'row', 'col')
- hyper_out: float32 [2, 2], replicated
- velocity_out: float32 [2, 2], replicated
The draws below stay inside these ranges and needn't reach their ends.
All inputs are finite; a program needn't handle non-finite values.
Results may differ from the reference program's by a relative error of at most 0.0001.
Values sent between devices are 32-bit elements; how exact they have to be, the bound alone decides.
No kernel may reach another device: no remote copies, remote signals or barrier semaphores. Data moves between devices by JAX's collectives and lax.ppermute only.
A program may use at most 64 MiB of HBM per device.

```python
import math
import jax
import jax.numpy as jnp
from jax import lax

CHAINS = 2
STEPS = 10
NR = 2048
NC = 4096


def draw_latent(key, part):
    values = jax.random.uniform(key, (CHAINS, NR, NC), jnp.float32, -3.0, 3.0)
    return values


def draw_counts(key, part):
    columns = jnp.arange(NC, dtype=jnp.int32)
    ceiling = jnp.broadcast_to(3 + 6 * columns // NC, (NR, NC))
    return jax.random.randint(key, (NR, NC), 0, ceiling, dtype=jnp.int32)


def levels(stream_key, extent, cuts, low, high):
    level = 1.0
    for position, blocks in cuts:
        draws = jax.random.uniform(jax.random.fold_in(jax.random.fold_in(stream_key, 6), position), (blocks,), jnp.float32, low / len(cuts), high / len(cuts))
        level = level * jnp.repeat(jnp.exp(draws), extent[position] // blocks).reshape((-1,) + (1,) * (len(extent) - 1 - position))
    return level


def bell_draw(rng, extent, scale, bound, held_as=jnp.bfloat16):
    array = jax.random.normal(rng, extent, jnp.float32) * scale
    return jnp.minimum(jnp.maximum(array, -bound), bound).astype(held_as)


def setup_inputs(seed: int = 0) -> dict:
    seeds = jax.random.split(jax.random.key(seed), 8)
    latent = draw_latent(jax.random.fold_in(seeds[7], 71), 0)
    momentum = jnp.clip(jax.random.uniform(seeds[1], (CHAINS, NR, NC), jnp.float32, -4.0, 4.0) * levels(seeds[1], (CHAINS, NR, NC), ((1, 8), (2, 16)), -0.4, 0.0), -4.0, 4.0)
    hyper_params = jnp.clip(jax.random.uniform(seeds[2], (2, CHAINS), jnp.float32, 0.3, 0.7), 0.3, 0.7)
    velocity = bell_draw(seeds[3], (2, CHAINS), 0.3, 3.0, jnp.float32)
    step_size = jnp.clip(jnp.exp(jax.random.uniform(seeds[4], (CHAINS,), jnp.float32, math.log(0.08), math.log(0.12))), 0.08, 0.12)
    counts = draw_counts(jax.random.fold_in(seeds[7], 71), 0)
    kappa_field = jnp.clip(jnp.exp(math.log(1.0) - 2.3025851 * jax.random.uniform(seeds[6], (NR, NC), jnp.float32) ** levels(seeds[6], (NR, NC), ((0, 8), (1, 16)), -0.2, 0.2)), 0.1, 1.0)
    return {"latent": latent, "momentum": momentum, "hyper_params": hyper_params, "velocity": velocity, "step_size": step_size, "counts": counts, "kappa_field": kappa_field}


def stencil(field):
    return jnp.roll(field, 1, 0) + jnp.roll(field, -1, 0) + jnp.roll(field, 1, 1) + jnp.roll(field, -1, 1)


def reference(latent, momentum, hyper_params, velocity, step_size, counts, kappa_field):
    count_float = counts.astype(jnp.float32)
    total = float(NR * NC)

    def gradient_at(field, params):
        tau_value = jnp.exp(params[1])
        applied = (kappa_field + 4.0) * field - stencil(field)
        intensity = jnp.exp(params[0] + field)
        gradient = tau_value * applied - count_float + intensity
        quadratic = jnp.sum(field * applied)
        excess = jnp.sum(intensity - count_float)
        accel = jnp.stack([excess / total, 0.5 * tau_value * quadratic / total - 0.5])
        return gradient, accel

    def single_chain(inputs):
        field, moment, params, speed, size_value = inputs
        gradient, accel = gradient_at(field, params)
        for index_step in range(STEPS):
            moment = moment - 0.5 * size_value * gradient
            speed = speed - 0.5 * size_value * accel
            field = field + size_value * moment
            params = params + size_value * speed
            gradient, accel = gradient_at(field, params)
            moment = moment - 0.5 * size_value * gradient
            speed = speed - 0.5 * size_value * accel
        return field, moment, params, speed

    results = lax.map(single_chain, (latent, momentum, hyper_params.T, velocity.T, step_size))
    return results[0], results[1], results[2].T, results[3].T
```

```python
import functools

import jax
import jax.numpy as jnp
from jax import lax
from jax.experimental import pallas as pl
from jax.experimental.pallas import tpu as pltpu
from jax.sharding import Mesh
from jax.sharding import PartitionSpec as P

STEPS = 10
ALL = ("row_0", "row_1", "col_0", "col_1", "col_2")
ROW = ("row_0", "row_1")
COL = ("col_0", "col_1", "col_2")

SIZE = 256
HALO = 16
GUARD = 8
TOP = GUARD + HALO
ROWS = 2 * TOP + SIZE
END = TOP + SIZE
FIELDS = 6
SHIFT = 8.0
VMEM = pl.BlockSpec(memory_space=pltpu.VMEM)
ANY = pl.BlockSpec(memory_space=pl.ANY)
F32 = jnp.float32
UNROLL = 2


def lanes():
    return lax.broadcasted_iota(jnp.int32, (8, 128), 1)


def splat(pair, chain):
    return jnp.broadcast_to(pair[:, chain : chain + 1], (8, 128))


def shifted(tiles, lane):
    right = [pltpu.roll(t, 127, 1) for t in tiles]
    left = [pltpu.roll(t, 1, 1) for t in tiles]
    last, first = lane == 127, lane == 0
    return [
        jnp.where(last, right[(i + 1) % 3], right[i]) + jnp.where(first, left[(i + 2) % 3], left[i])
        for i in range(3)
    ]


def applied(field, kappa, chain, row, lane, tiles):
    center = [field[chain, i, pl.ds(row, 8), :] for i in range(3)]
    beside = shifted(center, lane)
    result = []
    for i in range(tiles):
        around = beside[i] + (
            field[chain, i, pl.ds(row - 1, 8), :] + field[chain, i, pl.ds(row + 1, 8), :]
        )
        result.append((kappa[i, pl.ds(row, 8), :] + 4.0) * center[i] - around)
    return center, result


def loop(start, stop, body, init):
    def step(i, carry):
        return body(pl.multiple_of(start + 8 * i, 8), carry)

    return lax.fori_loop(0, (stop - start) // 8, step, init, unroll=UNROLL)


def advance(source, target, moment, counts, kappa, offset, tau, size, first_scale, sums):
    lane = lanes()
    offsets = [splat(offset, c) for c in range(2)]
    taus = [splat(tau, c) for c in range(2)]
    sizes = [splat(size, c) for c in range(2)]
    kicks = [first_scale * s for s in sizes]

    def body(row, carry, with_sums):
        carry = list(carry)
        count = [counts[i, pl.ds(row, 8), :] for i in range(3)]
        for c in range(2):
            center, result = applied(source, kappa, c, row, lane, 3)
            for i in range(3):
                intensity = jnp.exp(offsets[c] + center[i])
                gradient = taus[c] * result[i] - count[i] + intensity
                value = moment[c, i, pl.ds(row, 8), :] - kicks[c] * gradient
                moment[c, i, pl.ds(row, 8), :] = value
                target[c, i, pl.ds(row, 8), :] = center[i] + sizes[c] * value
                if with_sums and i < 2:
                    carry[c] += center[i] * result[i]
                    carry[2 + c] += intensity
        return tuple(carry)

    halo = functools.partial(body, with_sums=False)
    loop(GUARD, TOP, halo, ())
    loop(END, ROWS - GUARD, halo, ())
    if not sums:
        loop(TOP, END, halo, ())
        return None
    return loop(
        TOP, END, functools.partial(body, with_sums=True), (jnp.zeros((8, 128), F32),) * 4
    )


def sums_of(field, kappa, lead):
    lane = lanes()
    leads = [splat(lead, c) for c in range(2)]

    def body(row, carry):
        carry = list(carry)
        for c in range(2):
            center, result = applied(field, kappa, c, row, lane, 2)
            for i in range(2):
                carry[c] += center[i] * result[i]
                carry[2 + c] += jnp.exp(leads[c] + center[i])
        return tuple(carry)

    return loop(TOP, END, body, (jnp.zeros((8, 128), F32),) * 4)


def put_sums(out, values):
    lane = lax.broadcasted_iota(jnp.int32, (1, 8), 1)
    row = jnp.zeros((1, 8), F32)
    for i, value in enumerate(values):
        total = jnp.sum(jnp.sum(value, axis=0, keepdims=True), axis=1, keepdims=True)
        row = jnp.where(lane == i, total, row)
    out[...] = row


def start_kernel(
    latent, momentum, counts_in, kappa_in, offset,
    field, moment, counts, kappa, left, right, partial, raw, sems,
):
    copies = []
    for i in range(2):
        cols = pl.ds(128 * i, 128)
        own = pl.ds(TOP, SIZE)
        for c in range(2):
            copies.append((latent.at[c, :, cols], field.at[c, i, own, :]))
            copies.append((momentum.at[c, :, cols], moment.at[c, i, own, :]))
        copies.append((counts_in.at[:, cols], raw.at[i]))
        copies.append((kappa_in.at[:, cols], kappa.at[i, own, :]))
    copies = [pltpu.make_async_copy(a, b, sems.at[n]) for n, (a, b) in enumerate(copies)]
    for copy in copies:
        copy.start()
    for copy in copies:
        copy.wait()
    lane = lanes()
    group = lane // HALO
    offsets = [splat(offset[...], c) for c in range(2)]

    def body(row, carry):
        carry = list(carry)
        here = row - TOP
        for i in range(2):
            count = raw[i, pl.ds(pl.multiple_of(here, 8), 8), :].astype(F32)
            counts[i, pl.ds(row, 8), :] = count
            carry[4] += count
        for c in range(2):
            tiles = [field[c, i, pl.ds(row, 8), :] for i in range(2)]
            right0 = pltpu.roll(tiles[0], 127, 1)
            right1 = pltpu.roll(tiles[1], 127, 1)
            beside = [jnp.where(lane == 127, right1, right0), jnp.where(lane == 127, 0.0, right1)]
            for i in range(2):
                below = field[c, i, pl.ds(row + 1, 8), :]
                inside = lax.broadcasted_iota(jnp.int32, (8, 128), 0) + row < END - 1
                below = jnp.where(inside, below, 0.0)
                weight = (kappa[i, pl.ds(row, 8), :] + 4.0) * tiles[i]
                carry[c] += tiles[i] * (weight - 2.0 * (beside[i] + below))
                carry[2 + c] += jnp.exp(offsets[c] + tiles[i])
        for out, tile, base in ((left, 0, 0), (right, 1, HALO)):
            parts = [
                field[0, tile, pl.ds(row, 8), :],
                field[1, tile, pl.ds(row, 8), :],
                moment[0, tile, pl.ds(row, 8), :],
                moment[1, tile, pl.ds(row, 8), :],
                counts[tile, pl.ds(row, 8), :],
                kappa[tile, pl.ds(row, 8), :],
            ]
            packed = jnp.zeros((8, 128), F32)
            for n, part in enumerate(parts):
                shift = (HALO * n + base) % 128
                moved = part if shift == 0 else pltpu.roll(part, shift, 1)
                packed = jnp.where(group == n, moved, packed)
            out[pl.ds(pl.multiple_of(here, 8), 8), :] = packed
        return tuple(carry)

    totals = loop(TOP, END, body, (jnp.zeros((8, 128), F32),) * 5)
    put_sums(partial, totals)


def unpack(buffers, lane, n):
    from_right, from_left = buffers
    near = HALO * n % 128
    far = (HALO * n + HALO) % 128
    a = from_right if near == 0 else pltpu.roll(from_right, 128 - near, 1)
    b = from_left if far == 0 else pltpu.roll(from_left, 128 - far, 1)
    return jnp.where(lane < HALO, a, jnp.where(lane >= 128 - HALO, b, 0.0))


def parts_of(field, moment, counts, kappa):
    return [field.at[0], field.at[1], moment.at[0], moment.at[1], counts, kappa]


def columns_kernel(
    field_in, moment_in, counts_in, kappa_in, from_right, from_left, below, partial_in,
    field, moment, counts, kappa, up, down, partial,
):
    del field_in, moment_in, counts_in, kappa_in
    lane = lanes()
    parts = parts_of(field, moment, counts, kappa)

    def body(row, carry):
        carry = list(carry)
        here = pl.ds(pl.multiple_of(row - TOP, 8), 8)
        buffers = (from_right[here, :], from_left[here, :])
        for n, part in enumerate(parts):
            tile = unpack(buffers, lane, n)
            part[2, pl.ds(row, 8), :] = tile
            if n < 2:
                edge = pltpu.roll(part[1, pl.ds(row, 8), :], 1, 1) * tile
                carry[n] += jnp.where(lane == 0, edge, 0.0)
        return tuple(carry)

    edges = loop(TOP, END, body, (jnp.zeros((8, 128), F32),) * 2)
    for out, row, here in ((up, TOP, 0), (down, END - HALO, SIZE - HALO)):
        for n, part in enumerate(parts):
            for i in range(2):
                out[pl.ds(HALO * n, HALO), pl.ds(128 * i, 128)] = part[i, pl.ds(row, HALO), :]
        corner = pl.ds(HALO * FIELDS, HALO)
        out[corner, pl.ds(0, 128)] = from_right[pl.ds(here, HALO), :]
        out[corner, pl.ds(128, 128)] = from_left[pl.ds(here, HALO), :]
    totals = []
    for c in range(2):
        total = jnp.sum(jnp.sum(edges[c], axis=0, keepdims=True), axis=1, keepdims=True)
        for i in range(2):
            own = field[c, i, pl.ds(END - 1, 1), :]
            other = below[pl.ds(c, 1), pl.ds(128 * i, 128)]
            total += jnp.sum(own * other, axis=1, keepdims=True)
        totals.append(total)
    index = lax.broadcasted_iota(jnp.int32, (1, 8), 1)
    extra = jnp.where(index == 0, totals[0], jnp.where(index == 1, totals[1], 0.0))
    partial[...] = partial_in[...] - 2.0 * extra


def unpack_rows(from_above, from_below, field, moment, counts, kappa):
    lane = lanes()
    parts = parts_of(field, moment, counts, kappa)
    for buffer, row in ((from_above, GUARD), (from_below, END)):
        for block in range(0, HALO, 8):
            corner = pl.ds(HALO * FIELDS + block, 8)
            buffers = (buffer[corner, pl.ds(0, 128)], buffer[corner, pl.ds(128, 128)])
            for n, part in enumerate(parts):
                for i in range(2):
                    part[i, pl.ds(row + block, 8), :] = buffer[
                        pl.ds(HALO * n + block, 8), pl.ds(128 * i, 128)
                    ]
                part[2, pl.ds(row + block, 8), :] = unpack(buffers, lane, n)


OFFSET, SCALE, SPEED_0, SPEED_1, STEP, COUNT = range(6)


def read_table(table):
    return [table[pl.ds(i, 1), pl.ds(0, 2)] for i in range(6)]


def write_table(out, rows):
    out[...] = jnp.zeros((8, 128), F32)
    for i, row in enumerate(rows):
        out[pl.ds(i, 1), pl.ds(0, 2)] = row


def accel_of(quadratic, intensity, scale, count, total):
    return (intensity / total - count, 0.5 * jnp.exp(scale) * quadratic / total - 0.5)


def first_step_kernel(
    total, table, reduced, from_above, from_below, field_in, moment_in, counts_in, kappa_in,
    table_out, field, moment, counts, kappa, partial, other,
):
    del field_in, moment_in, counts_in, kappa_in
    unpack_rows(from_above, from_below, field, moment, counts, kappa)
    offset, scale, speed_0, speed_1, size, _ = read_table(table)
    quadratic, intensity = reduced[:, 0:2], reduced[:, 2:4]
    count = jnp.broadcast_to(reduced[:, 4:5], (1, 2)) / total
    a_0, a_1 = accel_of(quadratic, intensity, scale, count, total)
    advance(field, other, moment, counts, kappa, offset, jnp.exp(scale), size, 0.5, False)
    speed_0, speed_1 = speed_0 - 0.5 * size * a_0, speed_1 - 0.5 * size * a_1
    offset, scale = offset + size * speed_0, scale + size * speed_1
    near = advance(other, field, moment, counts, kappa, offset, jnp.exp(scale), size, 1.0, True)
    far = sums_of(field, kappa, offset - SHIFT)
    put_sums(partial, (*near, *far))
    write_table(table_out, (offset, scale, speed_0, speed_1, size, count))


def two_params(table, reduced, total):
    offset, scale, speed_0, speed_1, size, count = read_table(table)
    before = offset
    a_0, a_1 = accel_of(reduced[:, 0:2], reduced[:, 2:4], scale, count, total)
    speed_0, speed_1 = speed_0 - size * a_0, speed_1 - size * a_1
    offset, scale = offset + size * speed_0, scale + size * speed_1
    intensity = reduced[:, 6:8] * jnp.exp(offset - before + SHIFT)
    a_0, a_1 = accel_of(reduced[:, 4:6], intensity, scale, count, total)
    return offset, scale, speed_0, speed_1, size, count, a_0, a_1


def two_steps_kernel(
    total, table, reduced, field_in, moment_in, counts, kappa,
    table_out, field, moment, partial, other,
):
    del field_in, moment_in
    offset, scale, speed_0, speed_1, size, count, a_0, a_1 = two_params(table, reduced, total)
    advance(field, other, moment, counts, kappa, offset, jnp.exp(scale), size, 1.0, False)
    speed_0, speed_1 = speed_0 - size * a_0, speed_1 - size * a_1
    offset, scale = offset + size * speed_0, scale + size * speed_1
    near = advance(other, field, moment, counts, kappa, offset, jnp.exp(scale), size, 1.0, True)
    far = sums_of(field, kappa, offset - SHIFT)
    put_sums(partial, (*near, *far))
    write_table(table_out, (offset, scale, speed_0, speed_1, size, count))


def last_kernel(
    total, table, reduced, field, moment, counts, kappa,
    latent_out, momentum_out, hyper_out, velocity_out, result, sems,
):
    copies = []
    for c in range(2):
        for i in range(2):
            cols = pl.ds(128 * i, 128)
            copies.append((field.at[c, i, pl.ds(TOP, SIZE), :], latent_out.at[c, :, cols]))
    for c in range(2):
        for i in range(2):
            cols = pl.ds(128 * i, 128)
            copies.append((result.at[c, i], momentum_out.at[c, :, cols]))
    copies = [pltpu.make_async_copy(a, b, sems.at[n]) for n, (a, b) in enumerate(copies)]
    for copy in copies[:4]:
        copy.start()
    offset, scale, speed_0, speed_1, size, _, a_0, a_1 = two_params(table, reduced, total)
    lane = lanes()
    tau = jnp.exp(scale)
    for c in range(2):
        offset_c, tau_c, half = splat(offset, c), splat(tau, c), 0.5 * splat(size, c)

        def body(row, carry, c=c, offset_c=offset_c, tau_c=tau_c, half=half):
            center, applied_c = applied(field, kappa, c, row, lane, 2)
            here = pl.ds(pl.multiple_of(row - TOP, 8), 8)
            for i in range(2):
                gradient = tau_c * applied_c[i] - counts[i, pl.ds(row, 8), :]
                gradient += jnp.exp(offset_c + center[i])
                result[c, i, here, :] = moment[c, i, pl.ds(row, 8), :] - half * gradient
            return carry

        loop(TOP, END, body, ())
        for copy in copies[4 + 2 * c : 6 + 2 * c]:
            copy.start()
    hyper_out[pl.ds(0, 1), :] = offset
    hyper_out[pl.ds(1, 1), :] = scale
    velocity_out[pl.ds(0, 1), :] = speed_0 - 0.5 * size * a_0
    velocity_out[pl.ds(1, 1), :] = speed_1 - 0.5 * size * a_1
    for copy in copies:
        copy.wait()


def vmem(*shape):
    return pltpu.VMEM(shape, F32)


def held(*arrays):
    return tuple(pltpu.with_memory_space_constraint(a, pltpu.VMEM) for a in arrays)


STATE = (vmem(2, 3, ROWS, 128), vmem(2, 3, ROWS, 128), vmem(3, ROWS, 128), vmem(3, ROWS, 128))
PARAMS = pltpu.CompilerParams(vmem_limit_bytes=32 << 20)


def ring(x, axes, step):
    count = lax.axis_size(axes)
    return lax.ppermute(x, axes, [(i, (i + step) % count) for i in range(count)])


def all_sum(partial):
    count = lax.axis_size(ALL)
    spread = jnp.broadcast_to(partial[None], (count,) + partial.shape)
    return jnp.sum(lax.all_to_all(spread, ALL, 0, 0, tiled=True), axis=0)


def shards(latent, momentum, hyper_params, velocity, step_size, counts, kappa_field):
    total = float(latent.shape[1] * latent.shape[2] * lax.axis_size(ALL))
    below = ring(latent[:, 0, :], ROW, -1)
    table = jnp.zeros((8, 128), F32)
    rows = jnp.concatenate([hyper_params, velocity, step_size[None]], axis=0)
    table = lax.dynamic_update_slice(table, rows, (0, 0))
    buffer = jax.ShapeDtypeStruct((SIZE, 128), F32)
    small = jax.ShapeDtypeStruct((1, 8), F32)
    field, moment, count, kappa, left, right, partial = pl.pallas_call(
        start_kernel,
        out_shape=(*STATE, buffer, buffer, small),
        in_specs=[ANY] * 4 + [VMEM],
        out_specs=(VMEM,) * 7,
        scratch_shapes=[pltpu.VMEM((2, SIZE, 128), jnp.int32), pltpu.SemaphoreType.DMA((12,))],
        compiler_params=PARAMS,
        name="start",
    )(latent, momentum, counts, kappa_field, hyper_params[0:1])
    from_right, from_left = ring(left, COL, -1), ring(right, COL, 1)
    edge = jax.ShapeDtypeStruct((HALO * (FIELDS + 1), SIZE), F32)
    field, moment, count, kappa, up, down, partial = pl.pallas_call(
        columns_kernel,
        out_shape=(*STATE, edge, edge, small),
        in_specs=[VMEM] * 8,
        out_specs=(VMEM,) * 7,
        input_output_aliases={0: 0, 1: 1, 2: 2, 3: 3},
        compiler_params=PARAMS,
        name="columns",
    )(*held(field, moment, count, kappa), from_right, from_left, below, partial)
    from_below, from_above = ring(up, ROW, -1), ring(down, ROW, 1)
    reduced = all_sum(partial)
    small_table = jax.ShapeDtypeStruct((8, 128), F32)
    table, field, moment, count, kappa, partial = pl.pallas_call(
        functools.partial(first_step_kernel, total),
        out_shape=(small_table, *STATE, small),
        in_specs=[VMEM] * 8,
        out_specs=(VMEM,) * 6,
        input_output_aliases={4: 1, 5: 2, 6: 3, 7: 4},
        scratch_shapes=[vmem(2, 3, ROWS, 128)],
        compiler_params=PARAMS,
        name="first_steps",
    )(table, reduced, from_above, from_below, *held(field, moment, count, kappa))
    for _ in range(STEPS // 2 - 1):
        reduced = all_sum(partial)
        table, field, moment, partial = pl.pallas_call(
            functools.partial(two_steps_kernel, total),
            out_shape=(small_table, *STATE[:2], small),
            in_specs=[VMEM] * 6,
            out_specs=(VMEM,) * 4,
            input_output_aliases={2: 1, 3: 2},
            scratch_shapes=[vmem(2, 3, ROWS, 128)],
            compiler_params=PARAMS,
            name="two_steps",
        )(table, reduced, *held(field, moment, count, kappa))
    reduced = all_sum(partial)
    return pl.pallas_call(
        functools.partial(last_kernel, total),
        out_shape=(
            jax.ShapeDtypeStruct(latent.shape, F32),
            jax.ShapeDtypeStruct(latent.shape, F32),
            jax.ShapeDtypeStruct((2, 2), F32),
            jax.ShapeDtypeStruct((2, 2), F32),
        ),
        in_specs=[VMEM] * 6,
        out_specs=(ANY, ANY, VMEM, VMEM),
        scratch_shapes=[vmem(2, 2, SIZE, 128), pltpu.SemaphoreType.DMA((8,))],
        compiler_params=PARAMS,
        name="last",
    )(table, reduced, *held(field, moment, count, kappa))


def solution(mesh):
    torus = Mesh(mesh.devices.reshape(2, 4, 2, 4, 2), ALL)
    return jax.shard_map(
        shards,
        mesh=torus,
        in_specs=(P(None, ROW, COL), P(None, ROW, COL), P(), P(), P(), P(ROW, COL), P(ROW, COL)),
        out_specs=(P(None, ROW, COL), P(None, ROW, COL), P(), P()),
        check_vma=False,
    )
```

```python
import functools

import jax
import jax.numpy as jnp
from jax import lax
from jax.experimental import pallas as pl
from jax.experimental.pallas import tpu as pltpu
from jax.sharding import Mesh
from jax.sharding import PartitionSpec as P

STEPS = 10
ALL = ("row_0", "row_1", "col_0", "col_1", "col_2")
ROW = ("row_0", "row_1")
COL = ("col_0", "col_1", "col_2")

SIZE = 256
HALO = 16
GUARD = 8
TOP = GUARD + HALO
ROWS = 2 * TOP + SIZE
END = TOP + SIZE
FIELDS = 6
SHIFT = 8.0
VMEM = pl.BlockSpec(memory_space=pltpu.VMEM)
ANY = pl.BlockSpec(memory_space=pl.ANY)
F32 = jnp.float32
UNROLL = 16


def views(state):
    field, moment, slope, growth = (state.at[pl.ds(2 * i, 2)] for i in range(4))
    return field, moment, state.at[8], state.at[9], slope, growth


def lanes():
    return lax.broadcasted_iota(jnp.int32, (8, 128), 1)


def splat(pair, chain):
    return jnp.broadcast_to(pair[:, chain : chain + 1], (8, 128))


def shifted(tiles, lane):
    right = [pltpu.roll(t, 127, 1) for t in tiles]
    left = [pltpu.roll(t, 1, 1) for t in tiles]
    last, first = lane == 127, lane == 0
    return [
        jnp.where(last, right[(i + 1) % 3], right[i]) + jnp.where(first, left[(i + 2) % 3], left[i])
        for i in range(3)
    ]


def applied(field, kappa, chain, row, lane, tiles):
    center = [field[chain, i, pl.ds(row, 8), :] for i in range(3)]
    beside = shifted(center, lane)
    result = []
    for i in range(tiles):
        around = beside[i] + (
            field[chain, i, pl.ds(row - 1, 8), :] + field[chain, i, pl.ds(row + 1, 8), :]
        )
        result.append(kappa[i, pl.ds(row, 8), :] * center[i] - around)
    return center, result


def loop(start, stop, body, init):
    def step(i, carry):
        return body(pl.multiple_of(start + 8 * i, 8), carry)

    return lax.fori_loop(0, (stop - start) // 8, step, init, unroll=UNROLL)


def sweep(body, carry, depth):
    for start in (TOP - depth, END):
        loop(start, start + depth, lambda row, _: body(row, None) or (), ())
    return loop(TOP, END, body, carry)


def zeros(count):
    return (jnp.zeros((8, 128), F32),) * count


def advance(source, target, moment, counts, kappa, offset, tau, size, first_scale, depth):
    lane = lanes()
    offsets = [splat(offset, c) for c in range(2)]
    taus = [splat(tau, c) for c in range(2)]
    sizes = [splat(size, c) for c in range(2)]
    kicks = [first_scale * s for s in sizes]

    def body(row, carry):
        carry = carry and list(carry)
        count = [counts[i, pl.ds(row, 8), :] for i in range(3)]
        for c in range(2):
            center, result = applied(source, kappa, c, row, lane, 3)
            for i in range(3):
                intensity = jnp.exp(offsets[c] + center[i])
                gradient = taus[c] * result[i] - count[i] + intensity
                value = moment[c, i, pl.ds(row, 8), :] - kicks[c] * gradient
                moment[c, i, pl.ds(row, 8), :] = value
                target[c, i, pl.ds(row, 8), :] = center[i] + sizes[c] * value
                if carry and i < 2:
                    carry[c] += center[i] * result[i]
                    carry[2 + c] += intensity
        return carry and tuple(carry)

    return sweep(body, zeros(4), depth)


def advance_known(source, target, moment, counts, slope, growth, factor, tau, size, depth):
    factors = [splat(factor, c) for c in range(2)]
    taus = [splat(tau, c) for c in range(2)]
    sizes = [splat(size, c) for c in range(2)]

    def body(row, carry):
        here = pl.ds(row, 8)
        count = [counts[i, here, :] for i in range(3)]
        for c in range(2):
            for i in range(3):
                gradient = taus[c] * slope[c, i, here, :] - count[i]
                gradient += factors[c] * growth[c, i, here, :]
                value = moment[c, i, here, :] - sizes[c] * gradient
                moment[c, i, here, :] = value
                target[c, i, here, :] = source[c, i, here, :] + sizes[c] * value
        return carry

    loop(TOP - depth, END + depth, body, ())


def examine(field, kappa, slope, growth, lead, depth):
    lane = lanes()
    leads = [splat(lead, c) for c in range(2)]

    def body(row, carry):
        carry = carry and list(carry)
        for c in range(2):
            center, result = applied(field, kappa, c, row, lane, 3)
            for i in range(3):
                power = jnp.exp(leads[c] + center[i])
                slope[c, i, pl.ds(row, 8), :] = result[i]
                growth[c, i, pl.ds(row, 8), :] = power
                if carry and i < 2:
                    carry[c] += center[i] * result[i]
                    carry[2 + c] += power
        return carry and tuple(carry)

    return sweep(body, zeros(4), depth)


def put_sums(out, values):
    lane = lax.broadcasted_iota(jnp.int32, (1, 8), 1)
    row = jnp.zeros((1, 8), F32)
    for i, value in enumerate(values):
        total = jnp.sum(jnp.sum(value, axis=0, keepdims=True), axis=1, keepdims=True)
        row = jnp.where(lane == i, total, row)
    out[...] = jnp.broadcast_to(row[None], out.shape)


OFFSET, SCALE, SPEED_0, SPEED_1, STEP, COUNT = range(6)


def load_kernel(
    latent, momentum, counts_in, kappa_in, hyper, speed, size,
    state, left, right, low, table, raw, small, sems,
):
    field, moment, counts, kappa, _, _ = views(state)
    copies = [(hyper, small.at[pl.ds(0, 2)]), (speed, small.at[pl.ds(2, 2)])]
    copies.append((size, small.at[pl.ds(4, 1)]))
    for i in range(2):
        cols = pl.ds(128 * i, 128)
        own = pl.ds(TOP, SIZE)
        for c in range(2):
            copies.append((latent.at[c, :, cols], field.at[c, i, own, :]))
            copies.append((momentum.at[c, :, cols], moment.at[c, i, own, :]))
        copies.append((counts_in.at[:, cols], raw.at[i]))
        copies.append((kappa_in.at[:, cols], kappa.at[i, own, :]))
    copies = [pltpu.make_async_copy(a, b, sems.at[n]) for n, (a, b) in enumerate(copies)]
    for copy in copies:
        copy.start()
    for copy in copies:
        copy.wait()
    lane = lanes()
    group = lane // HALO

    def body(row, carry):
        here = pl.ds(pl.multiple_of(row - TOP, 8), 8)
        own = pl.ds(row, 8)
        for out, tile, base in ((left, 0, 0), (right, 1, HALO)):
            count = raw[tile, here, :].astype(F32)
            counts[tile, own, :] = count
            diagonal = kappa[tile, own, :] + 4.0
            kappa[tile, own, :] = diagonal
            parts = [
                field[0, tile, own, :],
                field[1, tile, own, :],
                moment[0, tile, own, :],
                moment[1, tile, own, :],
                count,
                diagonal,
            ]
            packed = jnp.zeros((8, 128), F32)
            for n, part in enumerate(parts):
                shift = (HALO * n + base) % 128
                moved = part if shift == 0 else pltpu.roll(part, shift, 1)
                packed = jnp.where(group == n, moved, packed)
            out[here, :] = packed
        return carry

    loop(TOP, END, body, ())
    for c in range(2):
        for i in range(2):
            low[pl.ds(c, 1), pl.ds(128 * i, 128)] = field[c, i, pl.ds(TOP, 1), :]
    table[...] = jnp.zeros((8, 128), F32)
    table[pl.ds(0, 5), pl.ds(0, 2)] = small[...]


def local_sums_kernel(table, state, partial):
    field, _, counts, kappa, _, _ = views(state)
    lane = lanes()
    offset = table[pl.ds(OFFSET, 1), pl.ds(0, 2)]
    offsets = [splat(offset, c) for c in range(2)]

    def body(row, carry):
        carry = list(carry)
        inside = lax.broadcasted_iota(jnp.int32, (8, 128), 0) + row < END - 1
        for i in range(2):
            carry[4] += counts[i, pl.ds(row, 8), :]
        for c in range(2):
            tiles = [field[c, i, pl.ds(row, 8), :] for i in range(2)]
            right0 = pltpu.roll(tiles[0], 127, 1)
            right1 = pltpu.roll(tiles[1], 127, 1)
            beside = [jnp.where(lane == 127, right1, right0), jnp.where(lane == 127, 0.0, right1)]
            for i in range(2):
                below = jnp.where(inside, field[c, i, pl.ds(row + 1, 8), :], 0.0)
                weight = kappa[i, pl.ds(row, 8), :] * tiles[i]
                carry[c] += tiles[i] * (weight - 2.0 * (beside[i] + below))
                carry[2 + c] += jnp.exp(offsets[c] + tiles[i])
        return tuple(carry)

    put_sums(partial, loop(TOP, END, body, zeros(5)))


def edges_kernel(state, from_right, below, partial, spread):
    field = views(state)[0]
    lane = lanes()

    def body(row, carry):
        carry = list(carry)
        buffer = from_right[pl.ds(pl.multiple_of(row - TOP, 8), 8), :]
        for c in range(2):
            other = buffer if c == 0 else pltpu.roll(buffer, 128 - HALO * c, 1)
            edge = pltpu.roll(field[c, 1, pl.ds(row, 8), :], 1, 1) * other
            carry[c] += jnp.where(lane == 0, edge, 0.0)
        return tuple(carry)

    edges = loop(TOP, END, body, zeros(2))
    index = lax.broadcasted_iota(jnp.int32, (1, 8), 1)
    row = partial[0]
    for c in range(2):
        total = jnp.sum(jnp.sum(edges[c], axis=0, keepdims=True), axis=1, keepdims=True)
        for i in range(2):
            own = field[c, i, pl.ds(END - 1, 1), :]
            other = below[pl.ds(c, 1), pl.ds(128 * i, 128)]
            total += jnp.sum(own * other, axis=1, keepdims=True)
        row -= jnp.where(index == c, 2.0 * total, 0.0)
    spread[...] = jnp.broadcast_to(row[None], spread.shape)


def unpack(buffers, lane, n):
    from_right, from_left = buffers
    near = HALO * n % 128
    far = (HALO * n + HALO) % 128
    a = from_right if near == 0 else pltpu.roll(from_right, 128 - near, 1)
    b = from_left if far == 0 else pltpu.roll(from_left, 128 - far, 1)
    return jnp.where(lane < HALO, a, jnp.where(lane >= 128 - HALO, b, 0.0))


def parts_of(state):
    field, moment, counts, kappa, _, _ = views(state)
    return [field.at[0], field.at[1], moment.at[0], moment.at[1], counts, kappa]


def columns_kernel(state_in, from_right, from_left, state, up, down):
    del state_in
    lane = lanes()
    parts = parts_of(state)

    def body(row, carry):
        here = pl.ds(pl.multiple_of(row - TOP, 8), 8)
        buffers = (from_right[here, :], from_left[here, :])
        for n, part in enumerate(parts):
            part[2, pl.ds(row, 8), :] = unpack(buffers, lane, n)
        return carry

    loop(TOP, END, body, ())
    for out, row, here in ((up, TOP, 0), (down, END - HALO, SIZE - HALO)):
        for n, part in enumerate(parts):
            for i in range(2):
                out[pl.ds(HALO * n, HALO), pl.ds(128 * i, 128)] = part[i, pl.ds(row, HALO), :]
        corner = pl.ds(HALO * FIELDS, HALO)
        out[corner, pl.ds(0, 128)] = from_right[pl.ds(here, HALO), :]
        out[corner, pl.ds(128, 128)] = from_left[pl.ds(here, HALO), :]


def unpack_rows(from_above, from_below, state):
    lane = lanes()
    parts = parts_of(state)
    for buffer, row in ((from_above, GUARD), (from_below, END)):
        for block in range(0, HALO, 8):
            corner = pl.ds(HALO * FIELDS + block, 8)
            buffers = (buffer[corner, pl.ds(0, 128)], buffer[corner, pl.ds(128, 128)])
            for n, part in enumerate(parts):
                for i in range(2):
                    part[i, pl.ds(row + block, 8), :] = buffer[
                        pl.ds(HALO * n + block, 8), pl.ds(128 * i, 128)
                    ]
                part[2, pl.ds(row + block, 8), :] = unpack(buffers, lane, n)


def sum_of(received):
    return jnp.sum(received[...], axis=0)


def read_table(table):
    return [table[pl.ds(i, 1), pl.ds(0, 2)] for i in range(6)]


def write_table(out, rows):
    out[...] = jnp.zeros((8, 128), F32)
    for i, row in enumerate(rows):
        out[pl.ds(i, 1), pl.ds(0, 2)] = row


def accel_of(quadratic, intensity, scale, count, total):
    return (intensity / total - count, 0.5 * jnp.exp(scale) * quadratic / total - 0.5)


def first_step_kernel(
    total, table, received, from_above, from_below, state_in, table_out, state, partial, other
):
    del state_in
    unpack_rows(from_above, from_below, state)
    field, moment, counts, kappa, slope, growth = views(state)
    reduced = sum_of(received)
    offset, scale, speed_0, speed_1, size, _ = read_table(table)
    quadratic, intensity = reduced[:, 0:2], reduced[:, 2:4]
    count = jnp.broadcast_to(reduced[:, 4:5], (1, 2)) / total
    a_0, a_1 = accel_of(quadratic, intensity, scale, count, total)
    advance(field, other, moment, counts, kappa, offset, jnp.exp(scale), size, 0.5, HALO)
    speed_0, speed_1 = speed_0 - 0.5 * size * a_0, speed_1 - 0.5 * size * a_1
    offset, scale = offset + size * speed_0, scale + size * speed_1
    near = advance(other, field, moment, counts, kappa, offset, jnp.exp(scale), size, 1.0, HALO)
    far = examine(field, kappa, slope, growth, offset - SHIFT, HALO // 2)
    put_sums(partial, (*near, *far))
    write_table(table_out, (offset, scale, speed_0, speed_1, size, count))


def two_params(table, received, total):
    reduced = sum_of(received)
    offset, scale, speed_0, speed_1, size, count = read_table(table)
    before = offset
    a_0, a_1 = accel_of(reduced[:, 0:2], reduced[:, 2:4], scale, count, total)
    speed_0, speed_1 = speed_0 - size * a_0, speed_1 - size * a_1
    offset, scale = offset + size * speed_0, scale + size * speed_1
    factor = jnp.exp(offset - before + SHIFT)
    intensity = reduced[:, 6:8] * factor
    a_0, a_1 = accel_of(reduced[:, 4:6], intensity, scale, count, total)
    return offset, scale, speed_0, speed_1, size, count, a_0, a_1, factor


def two_steps_kernel(total, table, received, state_in, table_out, state, partial, other):
    del state_in
    field, moment, counts, kappa, slope, growth = views(state)
    offset, scale, speed_0, speed_1, size, count, a_0, a_1, factor = two_params(table, received, total)
    advance_known(
        field, other, moment, counts, slope, growth, factor, jnp.exp(scale), size, HALO // 2
    )
    speed_0, speed_1 = speed_0 - size * a_0, speed_1 - size * a_1
    offset, scale = offset + size * speed_0, scale + size * speed_1
    near = advance(other, field, moment, counts, kappa, offset, jnp.exp(scale), size, 1.0, HALO // 2)
    far = examine(field, kappa, slope, growth, offset - SHIFT, HALO // 2)
    put_sums(partial, (*near, *far))
    write_table(table_out, (offset, scale, speed_0, speed_1, size, count))


def last_kernel(
    total, table, received, state,
    latent_out, momentum_out, hyper_out, velocity_out, result, sems,
):
    field, moment, counts, _, slope, growth = views(state)
    copies = []
    for c in range(2):
        for i in range(2):
            cols = pl.ds(128 * i, 128)
            copies.append((field.at[c, i, pl.ds(TOP, SIZE), :], latent_out.at[c, :, cols]))
    for c in range(2):
        for i in range(2):
            cols = pl.ds(128 * i, 128)
            copies.append((result.at[c, i], momentum_out.at[c, :, cols]))
    copies = [pltpu.make_async_copy(a, b, sems.at[n]) for n, (a, b) in enumerate(copies)]
    for copy in copies[:4]:
        copy.start()
    offset, scale, speed_0, speed_1, size, _, a_0, a_1, factor = two_params(table, received, total)
    tau = jnp.exp(scale)
    for c in range(2):
        tau_c, factor_c, half = splat(tau, c), splat(factor, c), 0.5 * splat(size, c)

        def body(row, carry, c=c, tau_c=tau_c, factor_c=factor_c, half=half):
            here = pl.ds(row, 8)
            out = pl.ds(pl.multiple_of(row - TOP, 8), 8)
            for i in range(2):
                gradient = tau_c * slope[c, i, here, :] - counts[i, here, :]
                gradient += factor_c * growth[c, i, here, :]
                result[c, i, out, :] = moment[c, i, here, :] - half * gradient
            return carry

        loop(TOP, END, body, ())
        for copy in copies[4 + 2 * c : 6 + 2 * c]:
            copy.start()
    hyper_out[pl.ds(0, 1), :] = offset
    hyper_out[pl.ds(1, 1), :] = scale
    velocity_out[pl.ds(0, 1), :] = speed_0 - 0.5 * size * a_0
    velocity_out[pl.ds(1, 1), :] = speed_1 - 0.5 * size * a_1
    for copy in copies:
        copy.wait()


def vmem(*shape):
    return pltpu.VMEM(shape, F32)


def held(array):
    return pltpu.with_memory_space_constraint(array, pltpu.VMEM)


STATE = vmem(10, 3, ROWS, 128)
PARAMS = pltpu.CompilerParams(vmem_limit_bytes=8 << 20)


def ring(x, axes, step):
    count = lax.axis_size(axes)
    return lax.ppermute(x, axes, [(i, (i + step) % count) for i in range(count)])


def exchange(spread):
    return lax.all_to_all(spread, ALL, 0, 0, tiled=True)


def shards(latent, momentum, hyper_params, velocity, step_size, counts, kappa_field):
    devices = lax.axis_size(ALL)
    total = float(latent.shape[1] * latent.shape[2] * devices)
    spread = vmem(devices, 1, 8)
    small_table = jax.ShapeDtypeStruct((8, 128), F32)
    given = (latent, momentum, counts, kappa_field, hyper_params, velocity, step_size[None])
    state, left, right, low, table = pl.pallas_call(
        load_kernel,
        out_shape=(STATE, vmem(SIZE, 128), vmem(SIZE, 128), vmem(2, SIZE), vmem(8, 128)),
        in_specs=[ANY] * 7,
        out_specs=(VMEM,) * 5,
        scratch_shapes=[
            pltpu.VMEM((2, SIZE, 128), jnp.int32),
            vmem(5, 2),
            pltpu.SemaphoreType.DMA((15,)),
        ],
        compiler_params=PARAMS,
        name="load",
    )(*(pltpu.with_memory_space_constraint(a, pltpu.HBM) for a in given))
    from_right, from_left = ring(left, COL, -1), ring(right, COL, 1)
    below = ring(low, ROW, -1)
    partial = pl.pallas_call(
        local_sums_kernel,
        out_shape=vmem(1, 1, 8),
        in_specs=[VMEM] * 2,
        out_specs=VMEM,
        compiler_params=PARAMS,
        name="local_sums",
    )(held(table), held(state))
    partial = pl.pallas_call(
        edges_kernel,
        out_shape=spread,
        in_specs=[VMEM] * 4,
        out_specs=VMEM,
        compiler_params=PARAMS,
        name="edges",
    )(held(state), from_right, below, partial)
    edge = vmem(HALO * (FIELDS + 1), SIZE)
    state, up, down = pl.pallas_call(
        columns_kernel,
        out_shape=(STATE, edge, edge),
        in_specs=[VMEM] * 3,
        out_specs=(VMEM,) * 3,
        input_output_aliases={0: 0},
        compiler_params=PARAMS,
        name="columns",
    )(held(state), from_right, from_left)
    from_below, from_above = ring(up, ROW, -1), ring(down, ROW, 1)
    received = exchange(partial)
    table, state, partial = pl.pallas_call(
        functools.partial(first_step_kernel, total),
        out_shape=(small_table, STATE, spread),
        in_specs=[VMEM] * 5,
        out_specs=(VMEM,) * 3,
        input_output_aliases={4: 1},
        scratch_shapes=[vmem(2, 3, ROWS, 128)],
        compiler_params=PARAMS,
        name="first_steps",
    )(table, received, from_above, from_below, held(state))
    for _ in range(STEPS // 2 - 1):
        received = exchange(partial)
        table, state, partial = pl.pallas_call(
            functools.partial(two_steps_kernel, total),
            out_shape=(small_table, STATE, spread),
            in_specs=[VMEM] * 3,
            out_specs=(VMEM,) * 3,
            input_output_aliases={2: 1},
            scratch_shapes=[vmem(2, 3, ROWS, 128)],
            compiler_params=PARAMS,
            name="two_steps",
        )(table, received, held(state))
    received = exchange(partial)
    return pl.pallas_call(
        functools.partial(last_kernel, total),
        out_shape=(
            jax.ShapeDtypeStruct(latent.shape, F32),
            jax.ShapeDtypeStruct(latent.shape, F32),
            jax.ShapeDtypeStruct((2, 2), F32),
            jax.ShapeDtypeStruct((2, 2), F32),
        ),
        in_specs=[VMEM] * 3,
        out_specs=(ANY, ANY, VMEM, VMEM),
        scratch_shapes=[vmem(2, 2, SIZE, 128), pltpu.SemaphoreType.DMA((8,))],
        compiler_params=PARAMS,
        name="last",
    )(table, received, held(state))


def solution(mesh):
    torus = Mesh(mesh.devices.reshape(2, 4, 2, 4, 2), ALL)
    return jax.shard_map(
        shards,
        mesh=torus,
        in_specs=(P(None, ROW, COL), P(None, ROW, COL), P(), P(), P(), P(ROW, COL), P(ROW, COL)),
        out_specs=(P(None, ROW, COL), P(None, ROW, COL), P(), P()),
        check_vma=False,
    )
```

```python
import functools

import jax
import jax.numpy as jnp
from jax import lax
from jax.experimental import pallas as pl
from jax.experimental.pallas import tpu as pltpu
from jax.sharding import Mesh
from jax.sharding import PartitionSpec as P

STEPS = 10
ALL = ("row_0", "row_1", "col_0", "col_1", "col_2")
ROW = ("row_0", "row_1")
COL = ("col_0", "col_1", "col_2")

SIZE = 256
HALO = 16
GUARD = 8
TOP = GUARD + HALO
ROWS = 2 * TOP + SIZE
END = TOP + SIZE
FIELDS = 6
PIECES = 4
SHIFT = 8.0
VMEM = pl.BlockSpec(memory_space=pltpu.VMEM)
ANY = pl.BlockSpec(memory_space=pl.ANY)
F32 = jnp.float32


def views(state):
    field, moment, slope, growth = (state.at[pl.ds(2 * i, 2)] for i in range(4))
    return field, moment, state.at[8], state.at[9], slope, growth


def lanes():
    return lax.broadcasted_iota(jnp.int32, (8, 128), 1)


def splat(pair, chain):
    return jnp.broadcast_to(pair[:, chain : chain + 1], (8, 128))


def shifted(tiles, lane):
    right = [pltpu.roll(t, 127, 1) for t in tiles]
    left = [pltpu.roll(t, 1, 1) for t in tiles]
    last, first = lane == 127, lane == 0
    return [
        jnp.where(last, right[(i + 1) % 3], right[i]) + jnp.where(first, left[(i + 2) % 3], left[i])
        for i in range(3)
    ]


def applied(field, kappa, chain, row, lane, tiles):
    center = [field[chain, i, pl.ds(row, 8), :] for i in range(3)]
    beside = shifted(center, lane)
    result = []
    for i in range(tiles):
        around = beside[i] + (
            field[chain, i, pl.ds(row - 1, 8), :] + field[chain, i, pl.ds(row + 1, 8), :]
        )
        result.append(kappa[i, pl.ds(row, 8), :] * center[i] - around)
    return center, result


def loop(start, stop, body, init):
    for row in range(start, stop, 8):
        init = body(row, init)
    return init


def sweep(body, carry, depth):
    for start in (TOP - depth, END):
        loop(start, start + depth, lambda row, _: body(row, None) or (), ())
    return loop(TOP, END, body, carry)


def zeros(count):
    return (jnp.zeros((8, 128), F32),) * count


def advance(source, target, moment, counts, kappa, offset, tau, size, first_scale, depth):
    lane = lanes()
    offsets = [splat(offset, c) for c in range(2)]
    taus = [splat(tau, c) for c in range(2)]
    sizes = [splat(size, c) for c in range(2)]
    kicks = [first_scale * s for s in sizes]

    def body(row, carry):
        carry = carry and list(carry)
        count = [counts[i, pl.ds(row, 8), :] for i in range(3)]
        for c in range(2):
            center, result = applied(source, kappa, c, row, lane, 3)
            for i in range(3):
                intensity = jnp.exp(offsets[c] + center[i])
                gradient = taus[c] * result[i] - count[i] + intensity
                value = moment[c, i, pl.ds(row, 8), :] - kicks[c] * gradient
                moment[c, i, pl.ds(row, 8), :] = value
                target[c, i, pl.ds(row, 8), :] = center[i] + sizes[c] * value
                if carry and i < 2:
                    carry[c] += center[i] * result[i]
                    carry[2 + c] += intensity
        return carry and tuple(carry)

    return sweep(body, zeros(4), depth)


def advance_known(source, target, moment, counts, slope, growth, factor, tau, size, depth):
    factors = [splat(factor, c) for c in range(2)]
    taus = [splat(tau, c) for c in range(2)]
    sizes = [splat(size, c) for c in range(2)]

    def body(row, carry):
        here = pl.ds(row, 8)
        count = [counts[i, here, :] for i in range(3)]
        for c in range(2):
            for i in range(3):
                gradient = taus[c] * slope[c, i, here, :] - count[i]
                gradient += factors[c] * growth[c, i, here, :]
                value = moment[c, i, here, :] - sizes[c] * gradient
                moment[c, i, here, :] = value
                target[c, i, here, :] = source[c, i, here, :] + sizes[c] * value
        return carry

    loop(TOP - depth, END + depth, body, ())


def examine(field, kappa, slope, growth, lead, depth):
    lane = lanes()
    leads = [splat(lead, c) for c in range(2)]

    def body(row, carry):
        carry = carry and list(carry)
        for c in range(2):
            center, result = applied(field, kappa, c, row, lane, 3)
            for i in range(3):
                power = jnp.exp(leads[c] + center[i])
                slope[c, i, pl.ds(row, 8), :] = result[i]
                growth[c, i, pl.ds(row, 8), :] = power
                if carry and i < 2:
                    carry[c] += center[i] * result[i]
                    carry[2 + c] += power
        return carry and tuple(carry)

    return sweep(body, zeros(4), depth)


def put_sums(out, values):
    lane = lax.broadcasted_iota(jnp.int32, (1, 8), 1)
    row = jnp.zeros((1, 8), F32)
    for i, value in enumerate(values):
        total = jnp.sum(jnp.sum(value, axis=0, keepdims=True), axis=1, keepdims=True)
        row = jnp.where(lane == i, total, row)
    out[...] = jnp.broadcast_to(row[None], out.shape)


OFFSET, SCALE, SPEED_0, SPEED_1, STEP, COUNT = range(6)


def load_kernel(
    latent, momentum, counts_in, kappa_in, hyper, speed, size,
    state, left, right, low, table, raw, small, sems,
):
    field, moment, counts, kappa, _, _ = views(state)
    copies = [(hyper, small.at[pl.ds(0, 2)]), (speed, small.at[pl.ds(2, 2)])]
    copies.append((size, small.at[pl.ds(4, 1)]))
    for i in range(2):
        cols = pl.ds(128 * i, 128)
        own = pl.ds(TOP, SIZE)
        for c in range(2):
            copies.append((latent.at[c, :, cols], field.at[c, i, own, :]))
            copies.append((momentum.at[c, :, cols], moment.at[c, i, own, :]))
        copies.append((counts_in.at[:, cols], raw.at[i]))
        copies.append((kappa_in.at[:, cols], kappa.at[i, own, :]))
    copies = [pltpu.make_async_copy(a, b, sems.at[n]) for n, (a, b) in enumerate(copies)]
    for copy in copies:
        copy.start()
    for copy in copies:
        copy.wait()
    lane = lanes()
    group = lane // HALO

    def body(row, carry):
        here = pl.ds(row - TOP, 8)
        own = pl.ds(row, 8)
        for out, tile, base in ((left, 0, 0), (right, 1, HALO)):
            count = raw[tile, here, :].astype(F32)
            counts[tile, own, :] = count
            diagonal = kappa[tile, own, :] + 4.0
            kappa[tile, own, :] = diagonal
            parts = [
                field[0, tile, own, :],
                field[1, tile, own, :],
                moment[0, tile, own, :],
                moment[1, tile, own, :],
                count,
                diagonal,
            ]
            packed = jnp.zeros((8, 128), F32)
            for n, part in enumerate(parts):
                shift = (HALO * n + base) % 128
                moved = part if shift == 0 else pltpu.roll(part, shift, 1)
                packed = jnp.where(group == n, moved, packed)
            out[here, :] = packed
        return carry

    loop(TOP, END, body, ())
    for c in range(2):
        for i in range(2):
            low[pl.ds(c, 1), pl.ds(128 * i, 128)] = field[c, i, pl.ds(TOP, 1), :]
    table[...] = jnp.zeros((8, 128), F32)
    table[pl.ds(0, 5), pl.ds(0, 2)] = small[...]


def local_sums_kernel(table, state, partial):
    field, _, counts, kappa, _, _ = views(state)
    lane = lanes()
    offset = table[pl.ds(OFFSET, 1), pl.ds(0, 2)]
    offsets = [splat(offset, c) for c in range(2)]

    def body(row, carry):
        carry = list(carry)
        inside = lax.broadcasted_iota(jnp.int32, (8, 128), 0) + row < END - 1
        for i in range(2):
            carry[4] += counts[i, pl.ds(row, 8), :]
        for c in range(2):
            tiles = [field[c, i, pl.ds(row, 8), :] for i in range(2)]
            right0 = pltpu.roll(tiles[0], 127, 1)
            right1 = pltpu.roll(tiles[1], 127, 1)
            beside = [jnp.where(lane == 127, right1, right0), jnp.where(lane == 127, 0.0, right1)]
            for i in range(2):
                below = jnp.where(inside, field[c, i, pl.ds(row + 1, 8), :], 0.0)
                weight = kappa[i, pl.ds(row, 8), :] * tiles[i]
                carry[c] += tiles[i] * (weight - 2.0 * (beside[i] + below))
                carry[2 + c] += jnp.exp(offsets[c] + tiles[i])
        return tuple(carry)

    put_sums(partial, loop(TOP, END, body, zeros(5)))


def edges_kernel(state, from_right, below, partial, spread):
    field = views(state)[0]
    lane = lanes()

    def body(row, carry):
        carry = list(carry)
        buffer = from_right[pl.ds(row - TOP, 8), :]
        for c in range(2):
            other = buffer if c == 0 else pltpu.roll(buffer, 128 - HALO * c, 1)
            edge = pltpu.roll(field[c, 1, pl.ds(row, 8), :], 1, 1) * other
            carry[c] += jnp.where(lane == 0, edge, 0.0)
        return tuple(carry)

    edges = loop(TOP, END, body, zeros(2))
    index = lax.broadcasted_iota(jnp.int32, (1, 8), 1)
    row = partial[0]
    for c in range(2):
        total = jnp.sum(jnp.sum(edges[c], axis=0, keepdims=True), axis=1, keepdims=True)
        for i in range(2):
            own = field[c, i, pl.ds(END - 1, 1), :]
            other = below[pl.ds(c, 1), pl.ds(128 * i, 128)]
            total += jnp.sum(own * other, axis=1, keepdims=True)
        row -= jnp.where(index == c, 2.0 * total, 0.0)
    spread[...] = jnp.broadcast_to(row[None], spread.shape)


def unpack(buffers, lane, n):
    from_right, from_left = buffers
    near = HALO * n % 128
    far = (HALO * n + HALO) % 128
    a = from_right if near == 0 else pltpu.roll(from_right, 128 - near, 1)
    b = from_left if far == 0 else pltpu.roll(from_left, 128 - far, 1)
    return jnp.where(lane < HALO, a, jnp.where(lane >= 128 - HALO, b, 0.0))


def parts_of(state):
    field, moment, counts, kappa, _, _ = views(state)
    return [field.at[0], field.at[1], moment.at[0], moment.at[1], counts, kappa]


def columns_kernel(state_in, from_right, from_left, state, up, down):
    del state_in
    lane = lanes()
    parts = parts_of(state)

    def body(row, carry):
        here = pl.ds(row - TOP, 8)
        buffers = (from_right[here, :], from_left[here, :])
        for n, part in enumerate(parts):
            part[2, pl.ds(row, 8), :] = unpack(buffers, lane, n)
        return carry

    loop(TOP, END, body, ())
    for out, row, here in ((up, TOP, 0), (down, END - HALO, SIZE - HALO)):
        for n, part in enumerate(parts):
            for i in range(2):
                out[pl.ds(HALO * n, HALO), pl.ds(128 * i, 128)] = part[i, pl.ds(row, HALO), :]
        corner = pl.ds(HALO * FIELDS, HALO)
        out[corner, pl.ds(0, 128)] = from_right[pl.ds(here, HALO), :]
        out[corner, pl.ds(128, 128)] = from_left[pl.ds(here, HALO), :]


def unpack_rows(from_above, from_below, state):
    lane = lanes()
    parts = parts_of(state)
    for buffer, row in ((from_above, GUARD), (from_below, END)):
        for block in range(0, HALO, 8):
            corner = pl.ds(HALO * FIELDS + block, 8)
            buffers = (buffer[corner, pl.ds(0, 128)], buffer[corner, pl.ds(128, 128)])
            for n, part in enumerate(parts):
                for i in range(2):
                    part[i, pl.ds(row + block, 8), :] = buffer[
                        pl.ds(HALO * n + block, 8), pl.ds(128 * i, 128)
                    ]
                part[2, pl.ds(row + block, 8), :] = unpack(buffers, lane, n)


def sum_of(received):
    return jnp.sum(received[...], axis=0)


def read_table(table):
    return [table[pl.ds(i, 1), pl.ds(0, 2)] for i in range(6)]


def write_table(out, rows):
    out[...] = jnp.zeros((8, 128), F32)
    for i, row in enumerate(rows):
        out[pl.ds(i, 1), pl.ds(0, 2)] = row


def accel_of(quadratic, intensity, scale, count, total):
    return (intensity / total - count, 0.5 * jnp.exp(scale) * quadratic / total - 0.5)


def first_step_kernel(
    total, table, received, from_above, from_below, state_in, table_out, state, partial, other
):
    del state_in
    unpack_rows(from_above, from_below, state)
    field, moment, counts, kappa, slope, growth = views(state)
    reduced = sum_of(received)
    offset, scale, speed_0, speed_1, size, _ = read_table(table)
    quadratic, intensity = reduced[:, 0:2], reduced[:, 2:4]
    count = jnp.broadcast_to(reduced[:, 4:5], (1, 2)) / total
    a_0, a_1 = accel_of(quadratic, intensity, scale, count, total)
    advance(field, other, moment, counts, kappa, offset, jnp.exp(scale), size, 0.5, HALO)
    speed_0, speed_1 = speed_0 - 0.5 * size * a_0, speed_1 - 0.5 * size * a_1
    offset, scale = offset + size * speed_0, scale + size * speed_1
    near = advance(other, field, moment, counts, kappa, offset, jnp.exp(scale), size, 1.0, HALO)
    far = examine(field, kappa, slope, growth, offset - SHIFT, HALO // 2)
    put_sums(partial, (*near, *far))
    write_table(table_out, (offset, scale, speed_0, speed_1, size, count))


def two_params(table, received, total):
    reduced = sum_of(received)
    offset, scale, speed_0, speed_1, size, count = read_table(table)
    before = offset
    a_0, a_1 = accel_of(reduced[:, 0:2], reduced[:, 2:4], scale, count, total)
    speed_0, speed_1 = speed_0 - size * a_0, speed_1 - size * a_1
    offset, scale = offset + size * speed_0, scale + size * speed_1
    factor = jnp.exp(offset - before + SHIFT)
    intensity = reduced[:, 6:8] * factor
    a_0, a_1 = accel_of(reduced[:, 4:6], intensity, scale, count, total)
    return offset, scale, speed_0, speed_1, size, count, a_0, a_1, factor


def field_copies(field, out, sems):
    pairs = [(c, i) for c in range(2) for i in range(2)]
    return [
        pltpu.make_async_copy(
            field.at[c, i, pl.ds(TOP, SIZE), :], out.at[c, :, pl.ds(128 * i, 128)], sems.at[n]
        )
        for n, (c, i) in enumerate(pairs)
    ]


def two_steps_kernel(
    total, final, table, received, state_in, table_out, state, partial, *more
):
    del state_in
    *latent_out, other = more[: 1 + final]
    field, moment, counts, kappa, slope, growth = views(state)
    offset, scale, speed_0, speed_1, size, count, a_0, a_1, factor = two_params(table, received, total)
    advance_known(
        field, other, moment, counts, slope, growth, factor, jnp.exp(scale), size, HALO // 2
    )
    speed_0, speed_1 = speed_0 - size * a_0, speed_1 - size * a_1
    offset, scale = offset + size * speed_0, scale + size * speed_1
    near = advance(other, field, moment, counts, kappa, offset, jnp.exp(scale), size, 1.0, HALO // 2)
    copies = []
    if final:
        copies = field_copies(field, latent_out[0], more[-1])
        for copy in copies:
            copy.start()
    far = examine(field, kappa, slope, growth, offset - SHIFT, HALO // 2)
    put_sums(partial, (*near, *far))
    write_table(table_out, (offset, scale, speed_0, speed_1, size, count))
    for copy in copies:
        copy.wait()


def last_kernel(
    total, table, received, state, momentum_out, hyper_out, velocity_out, result, small, sems
):
    _, moment, counts, _, slope, growth = views(state)
    offset, scale, speed_0, speed_1, size, _, a_0, a_1, factor = two_params(table, received, total)
    tau = jnp.exp(scale)
    taus = [splat(tau, c) for c in range(2)]
    factors = [splat(factor, c) for c in range(2)]
    halves = [0.5 * splat(size, c) for c in range(2)]
    for i, row in enumerate(
        (offset, scale, speed_0 - 0.5 * size * a_0, speed_1 - 0.5 * size * a_1)
    ):
        small[i // 2, pl.ds(i % 2, 1), :] = row
    copies = [
        pltpu.make_async_copy(small.at[0], hyper_out, sems.at[2 * PIECES]),
        pltpu.make_async_copy(small.at[1], velocity_out, sems.at[2 * PIECES + 1]),
    ]
    for copy in copies:
        copy.start()
    for n in range(PIECES):
        start = n * SIZE // PIECES
        rows = pl.ds(start, SIZE // PIECES)
        for row in range(TOP + start, TOP + start + SIZE // PIECES, 8):
            here = pl.ds(row, 8)
            for i in range(2):
                count = counts[i, here, :]
                for c in range(2):
                    gradient = taus[c] * slope[c, i, here, :] - count
                    gradient += factors[c] * growth[c, i, here, :]
                    value = moment[c, i, here, :] - halves[c] * gradient
                    result[c, pl.ds(row - TOP, 8), pl.ds(128 * i, 128)] = value
        for c in range(2):
            copies.append(
                pltpu.make_async_copy(
                    result.at[c, rows, :], momentum_out.at[c, rows, :], sems.at[2 * n + c]
                )
            )
            copies[-1].start()
    for copy in copies:
        copy.wait()


def vmem(*shape):
    return pltpu.VMEM(shape, F32)


def held(array):
    return pltpu.with_memory_space_constraint(array, pltpu.VMEM)


STATE = vmem(10, 3, ROWS, 128)
PARAMS = pltpu.CompilerParams(vmem_limit_bytes=8 << 20)


def ring(x, axes, step):
    count = lax.axis_size(axes)
    return lax.ppermute(x, axes, [(i, (i + step) % count) for i in range(count)])


def exchange(spread):
    return lax.all_to_all(spread, ALL, 0, 0, tiled=True)


def shards(latent, momentum, hyper_params, velocity, step_size, counts, kappa_field):
    devices = lax.axis_size(ALL)
    total = float(latent.shape[1] * latent.shape[2] * devices)
    spread = vmem(devices, 1, 8)
    small_table = jax.ShapeDtypeStruct((8, 128), F32)
    given = (latent, momentum, counts, kappa_field, hyper_params, velocity, step_size[None])
    state, left, right, low, table = pl.pallas_call(
        load_kernel,
        out_shape=(STATE, vmem(SIZE, 128), vmem(SIZE, 128), vmem(2, SIZE), vmem(8, 128)),
        in_specs=[ANY] * 7,
        out_specs=(VMEM,) * 5,
        scratch_shapes=[
            pltpu.VMEM((2, SIZE, 128), jnp.int32),
            vmem(5, 2),
            pltpu.SemaphoreType.DMA((15,)),
        ],
        compiler_params=PARAMS,
        name="load",
    )(*(pltpu.with_memory_space_constraint(a, pltpu.HBM) for a in given))
    from_right, from_left = ring(left, COL, -1), ring(right, COL, 1)
    below = ring(low, ROW, -1)
    partial = pl.pallas_call(
        local_sums_kernel,
        out_shape=vmem(1, 1, 8),
        in_specs=[VMEM] * 2,
        out_specs=VMEM,
        compiler_params=PARAMS,
        name="local_sums",
    )(held(table), held(state))
    partial = pl.pallas_call(
        edges_kernel,
        out_shape=spread,
        in_specs=[VMEM] * 4,
        out_specs=VMEM,
        compiler_params=PARAMS,
        name="edges",
    )(held(state), from_right, below, partial)
    edge = vmem(HALO * (FIELDS + 1), SIZE)
    state, up, down = pl.pallas_call(
        columns_kernel,
        out_shape=(STATE, edge, edge),
        in_specs=[VMEM] * 3,
        out_specs=(VMEM,) * 3,
        input_output_aliases={0: 0},
        compiler_params=PARAMS,
        name="columns",
    )(held(state), from_right, from_left)
    from_below, from_above = ring(up, ROW, -1), ring(down, ROW, 1)
    received = exchange(partial)
    table, state, partial = pl.pallas_call(
        functools.partial(first_step_kernel, total),
        out_shape=(small_table, STATE, spread),
        in_specs=[VMEM] * 5,
        out_specs=(VMEM,) * 3,
        input_output_aliases={4: 1},
        scratch_shapes=[vmem(2, 3, ROWS, 128)],
        compiler_params=PARAMS,
        name="first_steps",
    )(table, received, from_above, from_below, held(state))
    latent_out = ()
    result = jax.ShapeDtypeStruct(latent.shape, F32)
    for index in range(STEPS // 2 - 1):
        received = exchange(partial)
        final = index == STEPS // 2 - 2
        table, state, partial, *latent_out = pl.pallas_call(
            functools.partial(two_steps_kernel, total, final),
            out_shape=(small_table, STATE, spread) + final * (result,),
            in_specs=[VMEM] * 3,
            out_specs=(VMEM,) * 3 + final * (ANY,),
            input_output_aliases={2: 1},
            scratch_shapes=[vmem(2, 3, ROWS, 128)] + final * [pltpu.SemaphoreType.DMA((4,))],
            compiler_params=PARAMS,
            name="two_steps",
        )(table, received, held(state))
    received = exchange(partial)
    momentum_out, hyper_out, velocity_out = pl.pallas_call(
        functools.partial(last_kernel, total),
        out_shape=(
            result,
            jax.ShapeDtypeStruct((2, 2), F32),
            jax.ShapeDtypeStruct((2, 2), F32),
        ),
        in_specs=[VMEM] * 3,
        out_specs=(ANY,) * 3,
        scratch_shapes=[
            vmem(*latent.shape),
            vmem(2, 2, 2),
            pltpu.SemaphoreType.DMA((2 * PIECES + 2,)),
        ],
        compiler_params=PARAMS,
        name="last",
    )(table, received, held(state))
    return latent_out[0], momentum_out, hyper_out, velocity_out


def solution(mesh):
    torus = Mesh(mesh.devices.reshape(2, 4, 2, 4, 2), ALL)
    return jax.shard_map(
        shards,
        mesh=torus,
        in_specs=(P(None, ROW, COL), P(None, ROW, COL), P(), P(), P(), P(ROW, COL), P(ROW, COL)),
        out_specs=(P(None, ROW, COL), P(None, ROW, COL), P(), P()),
        check_vma=False,
    )
```

```python
import functools

import jax
import jax.numpy as jnp
from jax import lax
from jax.experimental import pallas as pl
from jax.experimental.pallas import tpu as pltpu
from jax.sharding import Mesh
from jax.sharding import PartitionSpec as P

STEPS = 10
ALL = ("row_0", "row_1", "col_0", "col_1", "col_2")
ROW = ("row_0", "row_1")
COL = ("col_0", "col_1", "col_2")

SIZE = 256
HALO = 16
GUARD = 8
TOP = GUARD + HALO
ROWS = 2 * TOP + SIZE + 8
END = TOP + SIZE
DEPTHS = (12, 12, 10, 10, 10, 10)
STARTS = (0, 12, 24, 34, 44, 54)
HALF = SIZE // 2
STRIP = 72
PIECES = 4
SHIFT = 8.0
VMEM = pl.BlockSpec(memory_space=pltpu.VMEM)
ANY = pl.BlockSpec(memory_space=pl.ANY)
F32 = jnp.float32


def views(state):
    field, moment, slope, growth = (state.at[pl.ds(2 * i, 2)] for i in range(4))
    return field, moment, state.at[8], state.at[9], slope, growth


def lanes():
    return lax.broadcasted_iota(jnp.int32, (8, 128), 1)


def splat(pair, chain):
    return jnp.broadcast_to(pair[:, chain : chain + 1], (8, 128))


def shifted(tiles, lane):
    right = [pltpu.roll(t, 127, 1) for t in tiles]
    left = [pltpu.roll(t, 1, 1) for t in tiles]
    last, first = lane == 127, lane == 0
    return [
        jnp.where(last, right[(i + 1) % 3], right[i]) + jnp.where(first, left[(i + 2) % 3], left[i])
        for i in range(3)
    ]


def applied(field, kappa, chain, row, lane, tiles):
    center = [field[chain, i, pl.ds(row, 8), :] for i in range(3)]
    beside = shifted(center, lane)
    result = []
    for i in range(tiles):
        around = beside[i] + (
            field[chain, i, pl.ds(row - 1, 8), :] + field[chain, i, pl.ds(row + 1, 8), :]
        )
        result.append(kappa[i, pl.ds(row, 8), :] * center[i] - around)
    return center, result


def loop(start, stop, body, init):
    for row in range(start, stop, 8):
        init = body(row, init)
    return init


def sweep(body, carry, depth):
    for start in (TOP - depth, END):
        loop(start, start + depth, lambda row, _: body(row, None) or (), ())
    return loop(TOP, END, body, carry)


def zeros(count):
    return (jnp.zeros((8, 128), F32),) * count


def advance(source, target, moment, counts, kappa, offset, tau, size, first_scale, depth):
    lane = lanes()
    offsets = [splat(offset, c) for c in range(2)]
    taus = [splat(tau, c) for c in range(2)]
    sizes = [splat(size, c) for c in range(2)]
    kicks = [first_scale * s for s in sizes]

    def body(row, carry):
        carry = carry and list(carry)
        count = [counts[i, pl.ds(row, 8), :] for i in range(3)]
        for c in range(2):
            center, result = applied(source, kappa, c, row, lane, 3)
            for i in range(3):
                intensity = jnp.exp(offsets[c] + center[i])
                gradient = taus[c] * result[i] - count[i] + intensity
                value = moment[c, i, pl.ds(row, 8), :] - kicks[c] * gradient
                moment[c, i, pl.ds(row, 8), :] = value
                target[c, i, pl.ds(row, 8), :] = center[i] + sizes[c] * value
                if carry and i < 2:
                    carry[c] += center[i] * result[i]
                    carry[2 + c] += intensity
        return carry and tuple(carry)

    return sweep(body, zeros(4), depth)


def advance_known(source, target, moment, counts, slope, growth, factor, tau, size, depth):
    factors = [splat(factor, c) for c in range(2)]
    taus = [splat(tau, c) for c in range(2)]
    sizes = [splat(size, c) for c in range(2)]

    def body(row, carry):
        here = pl.ds(row, 8)
        count = [counts[i, here, :] for i in range(3)]
        for c in range(2):
            for i in range(3):
                gradient = taus[c] * slope[c, i, here, :] - count[i]
                gradient += factors[c] * growth[c, i, here, :]
                value = moment[c, i, here, :] - sizes[c] * gradient
                moment[c, i, here, :] = value
                target[c, i, here, :] = source[c, i, here, :] + sizes[c] * value
        return carry

    loop(TOP - depth, END + depth, body, ())


def examine(field, kappa, slope, growth, lead, depth):
    lane = lanes()
    leads = [splat(lead, c) for c in range(2)]

    def body(row, carry):
        carry = carry and list(carry)
        for c in range(2):
            center, result = applied(field, kappa, c, row, lane, 3)
            for i in range(3):
                power = jnp.exp(leads[c] + center[i])
                slope[c, i, pl.ds(row, 8), :] = result[i]
                growth[c, i, pl.ds(row, 8), :] = power
                if carry and i < 2:
                    carry[c] += center[i] * result[i]
                    carry[2 + c] += power
        return carry and tuple(carry)

    return sweep(body, zeros(4), depth)


def put_sums(out, values):
    lane = lax.broadcasted_iota(jnp.int32, (1, 128), 1)
    row = jnp.zeros((1, 128), F32)
    for i, value in enumerate(values):
        total = jnp.sum(jnp.sum(value, axis=0, keepdims=True), axis=1, keepdims=True)
        row = jnp.where(lane == i, total, row)
    out[...] = jnp.broadcast_to(row, out.shape)


OFFSET, SCALE, SPEED_0, SPEED_1, STEP, COUNT = range(6)


def turned(value, shift):
    return value if shift % 128 == 0 else pltpu.roll(value, shift % 128, 1)


def even_row():
    return lax.axis_index(ROW[-1]) % 2 == 0


def even_column():
    return lax.axis_index(COL[-1]) % 2 == 0


def pack_columns(parts, tile, row, lane):
    packed = jnp.zeros((8, 128), F32)
    for half in range(2):
        for part, depth, start in zip(parts, DEPTHS, STARTS, strict=True):
            first = 64 * half + start
            value = part[tile, pl.ds(TOP + HALF * half + row, 8), :]
            inside = (lane >= first) & (lane < first + depth)
            packed = jnp.where(inside, turned(value, first + tile * depth), packed)
    return packed


def pack_rows(out, parts, row, skips):
    for part, depth, start, skip in zip(parts, DEPTHS, STARTS, skips, strict=True):
        for i in range(2):
            out[pl.ds(start, depth), pl.ds(128 * i, 128)] = part[i, pl.ds(row + skip, depth), :]


def load_kernel(
    latent, momentum, counts_in, kappa_in, hyper, speed, size,
    state, inner, outer, low, table, raw, small, sems,
):
    field, moment, counts, kappa, _, _ = views(state)
    copies = [(hyper, small.at[pl.ds(0, 2)]), (speed, small.at[pl.ds(2, 2)])]
    copies.append((size, small.at[pl.ds(4, 1)]))
    for i in range(2):
        cols = pl.ds(128 * i, 128)
        own = pl.ds(TOP, SIZE)
        for c in range(2):
            copies.append((latent.at[c, :, cols], field.at[c, i, own, :]))
            copies.append((momentum.at[c, :, cols], moment.at[c, i, own, :]))
        copies.append((counts_in.at[:, cols], raw.at[i]))
        copies.append((kappa_in.at[:, cols], kappa.at[i, own, :]))
    copies = [pltpu.make_async_copy(a, b, sems.at[n]) for n, (a, b) in enumerate(copies)]
    for copy in copies:
        copy.start()
    for copy in copies:
        copy.wait()
    lane = lanes()
    parts = parts_of(state)

    def body(row, carry):
        here = pl.ds(row - TOP, 8)
        own = pl.ds(row, 8)
        for i in range(2):
            counts[i, own, :] = raw[i, here, :].astype(F32)
            kappa[i, own, :] += 4.0
        return carry

    loop(TOP, END, body, ())
    for c in range(2):
        for i in range(2):
            low[pl.ds(c, 1), pl.ds(128 * i, 128)] = field[c, i, pl.ds(TOP, 1), :]
    even = even_column()
    for row in range(0, HALF, 8):
        left, right = (pack_columns(parts, tile, row, lane) for tile in range(2))
        inner[pl.ds(row, 8), :] = jnp.where(even, right, left)
        outer[pl.ds(row, 8), :] = jnp.where(even, left, right)
    table[...] = jnp.zeros((8, 128), F32)
    table[pl.ds(0, 5), pl.ds(0, 2)] = small[...]


def local_sums_kernel(table, state, partial, up, down):
    field, _, counts, kappa, _, _ = views(state)
    lane = lanes()
    offset = table[pl.ds(OFFSET, 1), pl.ds(0, 2)]
    offsets = [splat(offset, c) for c in range(2)]

    def body(row, carry):
        carry = list(carry)
        inside = lax.broadcasted_iota(jnp.int32, (8, 128), 0) + row < END - 1
        for i in range(2):
            carry[4] += counts[i, pl.ds(row, 8), :]
        for c in range(2):
            tiles = [field[c, i, pl.ds(row, 8), :] for i in range(2)]
            right0 = pltpu.roll(tiles[0], 127, 1)
            right1 = pltpu.roll(tiles[1], 127, 1)
            beside = [jnp.where(lane == 127, right1, right0), jnp.where(lane == 127, 0.0, right1)]
            for i in range(2):
                below = jnp.where(inside, field[c, i, pl.ds(row + 1, 8), :], 0.0)
                weight = kappa[i, pl.ds(row, 8), :] * tiles[i]
                carry[c] += tiles[i] * (weight - 2.0 * (beside[i] + below))
                carry[2 + c] += jnp.exp(offsets[c] + tiles[i])
        return tuple(carry)

    put_sums(partial, loop(TOP, END, body, zeros(5)))
    pack_rows(up, parts_of(state), TOP, [0] * 6)
    pack_rows(down, parts_of(state), END - HALO, [HALO - depth for depth in DEPTHS])


def parts_of(state):
    field, moment, counts, kappa, _, _ = views(state)
    return [field.at[0], field.at[1], moment.at[0], moment.at[1], counts, kappa]


def unpack(from_right, from_left, lane, n, right_at, left_at):
    depth = DEPTHS[n]
    right = turned(from_right, -right_at - STARTS[n])
    left = turned(from_left, -depth - left_at - STARTS[n])
    return jnp.where(lane < depth, right, jnp.where(lane >= 128 - depth, left, 0.0))


def join_kernel(
    state_in, col_inner, col_outer, below, partial, up, down, state, spread, inner, outer
):
    del state_in
    even = even_column()
    lane = lanes()
    parts = parts_of(state)
    field = views(state)[0]
    edges = list(zeros(2))
    for half in range(2):
        for row in range(0, HALF, 8):
            a, b = col_inner[pl.ds(row, 8), :], col_outer[pl.ds(row, 8), :]
            right, left = jnp.where(even, a, b), jnp.where(even, b, a)
            own = pl.ds(TOP + HALF * half + row, 8)
            for n, part in enumerate(parts):
                tile = unpack(right, left, lane, n, 64 * half, 64 * half)
                part[2, own, :] = tile
                if n < 2:
                    edge = pltpu.roll(part[1, own, :], 1, 1) * tile
                    edges[n] += jnp.where(lane == 0, edge, 0.0)
    even_r = even_row()

    def put(rows, cols, high, low):
        inner[rows, cols] = jnp.where(even_r, low, high)
        outer[rows, cols] = jnp.where(even_r, high, low)

    for i in range(2):
        cols = pl.ds(128 * i, 128)
        for row in range(0, 64, 8):
            rows = pl.ds(row, 8)
            put(rows, cols, up[rows, cols], down[rows, cols])
        top, end = pl.ds(8 * i, 8), pl.ds(HALF - HALO + 8 * i, 8)
        (right, low_right), (left, low_left) = (
            [jnp.where(even, p[rows, :], q[rows, :]) for rows in (top, end)]
            for p, q in ((col_inner, col_outer), (col_outer, col_inner))
        )
        high = jnp.where(lane < 64, right, pltpu.roll(left, 64, 1))
        low = jnp.where(lane < 64, pltpu.roll(low_right, 64, 1), low_left)
        put(pl.ds(64, 8), cols, high, low)
    index = lax.broadcasted_iota(jnp.int32, (1, 128), 1)
    result = partial[pl.ds(0, 1), :]
    for c in range(2):
        total = jnp.sum(jnp.sum(edges[c], axis=0, keepdims=True), axis=1, keepdims=True)
        for i in range(2):
            own = field[c, i, pl.ds(END - 1, 1), :]
            other = below[pl.ds(c, 1), pl.ds(128 * i, 128)]
            total += jnp.sum(own * other, axis=1, keepdims=True)
        result -= jnp.where(index == c, 2.0 * total, 0.0)
    spread[...] = jnp.broadcast_to(result, spread.shape)


def unpack_rows(inner, outer, state):
    lane = lanes()
    parts = parts_of(state)
    even = even_row()

    def both(*at):
        a, b = inner[at], outer[at]
        return jnp.where(even, b, a), jnp.where(even, a, b)

    for n, (part, depth, start) in enumerate(zip(parts, DEPTHS, STARTS, strict=True)):
        for i in range(2):
            above, below = both(pl.ds(start, depth), pl.ds(128 * i, 128))
            part[i, pl.ds(TOP - depth, depth), :] = above
            part[i, pl.ds(END, depth), :] = below
    for i in range(2):
        above, below = both(pl.ds(64, 8), pl.ds(128 * i, 128))
        for n, part in enumerate(parts):
            part[2, pl.ds(GUARD + 8 * i, 8), :] = unpack(above, above, lane, n, 0, 64)
            part[2, pl.ds(END + 8 * i, 8), :] = unpack(below, below, lane, n, 0, 64)


def sum_of(received):
    return jnp.sum(received[...], axis=0, keepdims=True)


def read_table(table):
    return [table[pl.ds(i, 1), pl.ds(0, 2)] for i in range(6)]


def write_table(out, rows):
    out[...] = jnp.zeros((8, 128), F32)
    for i, row in enumerate(rows):
        out[pl.ds(i, 1), pl.ds(0, 2)] = row


def accel_of(quadratic, intensity, scale, count, total):
    return (intensity / total - count, 0.5 * jnp.exp(scale) * quadratic / total - 0.5)


def first_step_kernel(
    total, table, received, inner, outer, state_in, table_out, state, partial, other
):
    del state_in
    unpack_rows(inner, outer, state)
    field, moment, counts, kappa, slope, growth = views(state)
    reduced = sum_of(received)
    offset, scale, speed_0, speed_1, size, _ = read_table(table)
    quadratic, intensity = reduced[:, 0:2], reduced[:, 2:4]
    count = jnp.broadcast_to(reduced[:, 4:5], (1, 2)) / total
    a_0, a_1 = accel_of(quadratic, intensity, scale, count, total)
    advance(field, other, moment, counts, kappa, offset, jnp.exp(scale), size, 0.5, HALO)
    speed_0, speed_1 = speed_0 - 0.5 * size * a_0, speed_1 - 0.5 * size * a_1
    offset, scale = offset + size * speed_0, scale + size * speed_1
    near = advance(other, field, moment, counts, kappa, offset, jnp.exp(scale), size, 1.0, HALO)
    far = examine(field, kappa, slope, growth, offset - SHIFT, HALO // 2)
    put_sums(partial, (*near, *far))
    write_table(table_out, (offset, scale, speed_0, speed_1, size, count))


def two_params(table, received, total):
    reduced = sum_of(received)
    offset, scale, speed_0, speed_1, size, count = read_table(table)
    before = offset
    a_0, a_1 = accel_of(reduced[:, 0:2], reduced[:, 2:4], scale, count, total)
    speed_0, speed_1 = speed_0 - size * a_0, speed_1 - size * a_1
    offset, scale = offset + size * speed_0, scale + size * speed_1
    factor = jnp.exp(offset - before + SHIFT)
    intensity = reduced[:, 6:8] * factor
    a_0, a_1 = accel_of(reduced[:, 4:6], intensity, scale, count, total)
    return offset, scale, speed_0, speed_1, size, count, a_0, a_1, factor


def field_copies(field, out, sems):
    pairs = [(c, i) for c in range(2) for i in range(2)]
    return [
        pltpu.make_async_copy(
            field.at[c, i, pl.ds(TOP, SIZE), :], out.at[c, :, pl.ds(128 * i, 128)], sems.at[n]
        )
        for n, (c, i) in enumerate(pairs)
    ]


def two_steps_kernel(
    total, final, table, received, state_in, table_out, state, partial, *more
):
    del state_in
    *latent_out, other = more[: 1 + final]
    field, moment, counts, kappa, slope, growth = views(state)
    offset, scale, speed_0, speed_1, size, count, a_0, a_1, factor = two_params(table, received, total)
    advance_known(
        field, other, moment, counts, slope, growth, factor, jnp.exp(scale), size, HALO // 2
    )
    speed_0, speed_1 = speed_0 - size * a_0, speed_1 - size * a_1
    offset, scale = offset + size * speed_0, scale + size * speed_1
    near = advance(other, field, moment, counts, kappa, offset, jnp.exp(scale), size, 1.0, HALO // 2)
    copies = []
    if final:
        copies = field_copies(field, latent_out[0], more[-1])
        for copy in copies:
            copy.start()
    far = examine(field, kappa, slope, growth, offset - SHIFT, HALO // 2)
    put_sums(partial, (*near, *far))
    write_table(table_out, (offset, scale, speed_0, speed_1, size, count))
    for copy in copies:
        copy.wait()


def last_kernel(
    total, table, received, state, momentum_out, hyper_out, velocity_out, result, small, sems
):
    _, moment, counts, _, slope, growth = views(state)
    offset, scale, speed_0, speed_1, size, _, a_0, a_1, factor = two_params(table, received, total)
    tau = jnp.exp(scale)
    taus = [splat(tau, c) for c in range(2)]
    factors = [splat(factor, c) for c in range(2)]
    halves = [0.5 * splat(size, c) for c in range(2)]
    for i, row in enumerate(
        (offset, scale, speed_0 - 0.5 * size * a_0, speed_1 - 0.5 * size * a_1)
    ):
        small[i // 2, pl.ds(i % 2, 1), :] = row
    copies = [
        pltpu.make_async_copy(small.at[0], hyper_out, sems.at[2 * PIECES]),
        pltpu.make_async_copy(small.at[1], velocity_out, sems.at[2 * PIECES + 1]),
    ]
    for copy in copies:
        copy.start()
    for n in range(PIECES):
        start = n * SIZE // PIECES
        rows = pl.ds(start, SIZE // PIECES)
        for row in range(TOP + start, TOP + start + SIZE // PIECES, 8):
            here = pl.ds(row, 8)
            for i in range(2):
                count = counts[i, here, :]
                for c in range(2):
                    gradient = taus[c] * slope[c, i, here, :] - count
                    gradient += factors[c] * growth[c, i, here, :]
                    value = moment[c, i, here, :] - halves[c] * gradient
                    result[c, pl.ds(row - TOP, 8), pl.ds(128 * i, 128)] = value
        for c in range(2):
            copies.append(
                pltpu.make_async_copy(
                    result.at[c, rows, :], momentum_out.at[c, rows, :], sems.at[2 * n + c]
                )
            )
            copies[-1].start()
    for copy in copies:
        copy.wait()


def vmem(*shape):
    return pltpu.VMEM(shape, F32)


def held(array):
    return pltpu.with_memory_space_constraint(array, pltpu.VMEM)


STATE = vmem(10, 3, ROWS, 128)
PARAMS = pltpu.CompilerParams(vmem_limit_bytes=8 << 20)


def ring(x, axes, step):
    count = lax.axis_size(axes)
    return lax.ppermute(x, axes, [(i, (i + step) % count) for i in range(count)])


def swap(x, axes, first):
    count = lax.axis_size(axes)
    pairs = [((first + i) % count, (first + i + 1) % count) for i in range(0, count, 2)]
    return lax.ppermute(x, axes, [p for a, b in pairs for p in ((a, b), (b, a))])


def exchange(spread):
    shape = spread.shape
    spread = spread.reshape(shape[0], 1, shape[1])
    return lax.all_to_all(spread, ALL, 0, 0, tiled=True).reshape(shape)


def shards(latent, momentum, hyper_params, velocity, step_size, counts, kappa_field):
    devices = lax.axis_size(ALL)
    total = float(latent.shape[1] * latent.shape[2] * devices)
    spread = vmem(devices, 128)
    small_table = jax.ShapeDtypeStruct((8, 128), F32)
    given = (latent, momentum, counts, kappa_field, hyper_params, velocity, step_size[None])
    packed, strip = vmem(HALF, 128), vmem(STRIP, SIZE)
    state, inner, outer, low, table = pl.pallas_call(
        load_kernel,
        out_shape=(STATE, packed, packed, vmem(2, SIZE), vmem(8, 128)),
        in_specs=[ANY] * 7,
        out_specs=(VMEM,) * 5,
        scratch_shapes=[
            pltpu.VMEM((2, SIZE, 128), jnp.int32),
            vmem(5, 2),
            pltpu.SemaphoreType.DMA((15,)),
        ],
        compiler_params=PARAMS,
        name="load",
    )(*(pltpu.with_memory_space_constraint(a, pltpu.HBM) for a in given))
    below = ring(low, ROW, -1)
    inner, outer = swap(inner, COL, 0), swap(outer, COL, 1)
    partial, up, down = pl.pallas_call(
        local_sums_kernel,
        out_shape=(vmem(8, 128), strip, strip),
        in_specs=[VMEM] * 2,
        out_specs=(VMEM,) * 3,
        compiler_params=PARAMS,
        name="local_sums",
    )(held(table), held(state))
    state, partial, row_inner, row_outer = pl.pallas_call(
        join_kernel,
        out_shape=(STATE, spread, strip, strip),
        in_specs=[VMEM] * 7,
        out_specs=(VMEM,) * 4,
        input_output_aliases={0: 0},
        compiler_params=PARAMS,
        name="join",
    )(held(state), inner, outer, below, partial, held(up), held(down))
    row_inner, row_outer = swap(row_inner, ROW, 0), swap(row_outer, ROW, 1)
    received = exchange(partial)
    table, state, partial = pl.pallas_call(
        functools.partial(first_step_kernel, total),
        out_shape=(small_table, STATE, spread),
        in_specs=[VMEM] * 5,
        out_specs=(VMEM,) * 3,
        input_output_aliases={4: 1},
        scratch_shapes=[vmem(2, 3, ROWS, 128)],
        compiler_params=PARAMS,
        name="first_steps",
    )(table, received, row_inner, row_outer, held(state))
    latent_out = ()
    result = jax.ShapeDtypeStruct(latent.shape, F32)
    for index in range(STEPS // 2 - 1):
        received = exchange(partial)
        final = index == STEPS // 2 - 2
        table, state, partial, *latent_out = pl.pallas_call(
            functools.partial(two_steps_kernel, total, final),
            out_shape=(small_table, STATE, spread) + final * (result,),
            in_specs=[VMEM] * 3,
            out_specs=(VMEM,) * 3 + final * (ANY,),
            input_output_aliases={2: 1},
            scratch_shapes=[vmem(2, 3, ROWS, 128)] + final * [pltpu.SemaphoreType.DMA((4,))],
            compiler_params=PARAMS,
            name="two_steps",
        )(table, received, held(state))
    received = exchange(partial)
    momentum_out, hyper_out, velocity_out = pl.pallas_call(
        functools.partial(last_kernel, total),
        out_shape=(
            result,
            jax.ShapeDtypeStruct((2, 2), F32),
            jax.ShapeDtypeStruct((2, 2), F32),
        ),
        in_specs=[VMEM] * 3,
        out_specs=(ANY,) * 3,
        scratch_shapes=[
            vmem(*latent.shape),
            vmem(2, 2, 2),
            pltpu.SemaphoreType.DMA((2 * PIECES + 2,)),
        ],
        compiler_params=PARAMS,
        name="last",
    )(table, received, held(state))
    return latent_out[0], momentum_out, hyper_out, velocity_out


def solution(mesh):
    torus = Mesh(mesh.devices.reshape(2, 4, 2, 4, 2), ALL)
    return jax.shard_map(
        shards,
        mesh=torus,
        in_specs=(P(None, ROW, COL), P(None, ROW, COL), P(), P(), P(), P(ROW, COL), P(ROW, COL)),
        out_specs=(P(None, ROW, COL), P(None, ROW, COL), P(), P()),
        check_vma=False,
    )
```

```python
import functools

import jax
import jax.numpy as jnp
from jax import lax
from jax.experimental import pallas as pl
from jax.experimental.pallas import tpu as pltpu
from jax.sharding import Mesh
from jax.sharding import PartitionSpec as P

STEPS = 10
ALL = ("row_0", "row_1", "col_0", "col_1", "col_2")
ROW = ("row_0", "row_1")
COL = ("col_0", "col_1", "col_2")

SIZE = 256
HALO = 16
GUARD = 8
TOP = GUARD + HALO
ROWS = 2 * TOP + SIZE + 8
END = TOP + SIZE
DEPTHS = (12, 12, 10, 10, 10, 10)
STARTS = (0, 12, 24, 34, 44, 54)
HALF = SIZE // 2
STRIP = 72
PIECES = 4
SHIFT = 8.0
VMEM = pl.BlockSpec(memory_space=pltpu.VMEM)
ANY = pl.BlockSpec(memory_space=pl.ANY)
F32 = jnp.float32


def views(state):
    field, moment, slope, growth = (state.at[pl.ds(2 * i, 2)] for i in range(4))
    return field, moment, state.at[8], state.at[9], slope, growth


def lanes():
    return lax.broadcasted_iota(jnp.int32, (8, 128), 1)


def splat(pair, chain):
    return jnp.broadcast_to(pair[:, chain : chain + 1], (8, 128))


def shifted(tiles, lane):
    right = [pltpu.roll(t, 127, 1) for t in tiles]
    left = [pltpu.roll(t, 1, 1) for t in tiles]
    last, first = lane == 127, lane == 0
    return [
        jnp.where(last, right[(i + 1) % 3], right[i]) + jnp.where(first, left[(i + 2) % 3], left[i])
        for i in range(3)
    ]


def applied(field, kappa, chain, row, lane, tiles):
    center = [field[chain, i, pl.ds(row, 8), :] for i in range(3)]
    beside = shifted(center, lane)
    result = []
    for i in range(tiles):
        around = beside[i] + (
            field[chain, i, pl.ds(row - 1, 8), :] + field[chain, i, pl.ds(row + 1, 8), :]
        )
        result.append(kappa[i, pl.ds(row, 8), :] * center[i] - around)
    return center, result


def loop(start, stop, body, init):
    for row in range(start, stop, 8):
        init = body(row, init)
    return init


def sweep(body, carry, depth):
    for start in (TOP - depth, END):
        loop(start, start + depth, lambda row, _: body(row, None) or (), ())
    return loop(TOP, END, body, carry)


def zeros(count):
    return (jnp.zeros((8, 128), F32),) * count


def advance(source, target, moment, counts, kappa, offset, tau, size, first_scale, depth):
    lane = lanes()
    offsets = [splat(offset, c) for c in range(2)]
    taus = [splat(tau, c) for c in range(2)]
    sizes = [splat(size, c) for c in range(2)]
    kicks = [first_scale * s for s in sizes]

    def body(row, carry):
        carry = carry and list(carry)
        count = [counts[i, pl.ds(row, 8), :] for i in range(3)]
        for c in range(2):
            center, result = applied(source, kappa, c, row, lane, 3)
            for i in range(3):
                intensity = jnp.exp(offsets[c] + center[i])
                gradient = taus[c] * result[i] - count[i] + intensity
                value = moment[c, i, pl.ds(row, 8), :] - kicks[c] * gradient
                moment[c, i, pl.ds(row, 8), :] = value
                target[c, i, pl.ds(row, 8), :] = center[i] + sizes[c] * value
                if carry and i < 2:
                    carry[c] += center[i] * result[i]
                    carry[2 + c] += intensity
        return carry and tuple(carry)

    return sweep(body, zeros(4), depth)


def advance_known(source, target, moment, counts, slope, growth, factor, tau, size, depth):
    factors = [splat(factor, c) for c in range(2)]
    taus = [splat(tau, c) for c in range(2)]
    sizes = [splat(size, c) for c in range(2)]

    def body(row, carry):
        here = pl.ds(row, 8)
        count = [counts[i, here, :] for i in range(3)]
        for c in range(2):
            for i in range(3):
                gradient = taus[c] * slope[c, i, here, :] - count[i]
                gradient += factors[c] * growth[c, i, here, :]
                value = moment[c, i, here, :] - sizes[c] * gradient
                moment[c, i, here, :] = value
                target[c, i, here, :] = source[c, i, here, :] + sizes[c] * value
        return carry

    loop(TOP - depth, END + depth, body, ())


def examine(field, kappa, slope, growth, lead, depth):
    lane = lanes()
    leads = [splat(lead, c) for c in range(2)]

    def body(row, carry):
        carry = carry and list(carry)
        for c in range(2):
            center, result = applied(field, kappa, c, row, lane, 3)
            for i in range(3):
                power = jnp.exp(leads[c] + center[i])
                slope[c, i, pl.ds(row, 8), :] = result[i]
                growth[c, i, pl.ds(row, 8), :] = power
                if carry and i < 2:
                    carry[c] += center[i] * result[i]
                    carry[2 + c] += power
        return carry and tuple(carry)

    return sweep(body, zeros(4), depth)


def put_sums(out, values):
    lane = lax.broadcasted_iota(jnp.int32, (1, 128), 1)
    row = jnp.zeros((1, 128), F32)
    for i, value in enumerate(values):
        total = jnp.sum(jnp.sum(value, axis=0, keepdims=True), axis=1, keepdims=True)
        row = jnp.where(lane == i, total, row)
    out[...] = jnp.broadcast_to(row, out.shape)


OFFSET, SCALE, SPEED_0, SPEED_1, STEP, COUNT = range(6)


def turned(value, shift):
    return value if shift % 128 == 0 else pltpu.roll(value, shift % 128, 1)


def even_row():
    return lax.axis_index(ROW[-1]) % 2 == 0


def even_column():
    return lax.axis_index(COL[-1]) % 2 == 0


def pack_columns(parts, tile, row, lane):
    packed = jnp.zeros((8, 128), F32)
    for half in range(2):
        for part, depth, start in zip(parts, DEPTHS, STARTS, strict=True):
            first = 64 * half + start
            value = part[tile, pl.ds(TOP + HALF * half + row, 8), :]
            inside = (lane >= first) & (lane < first + depth)
            packed = jnp.where(inside, turned(value, first + tile * depth), packed)
    return packed


def pack_rows(out, parts, row, skips):
    for part, depth, start, skip in zip(parts, DEPTHS, STARTS, skips, strict=True):
        for i in range(2):
            out[pl.ds(start, depth), pl.ds(128 * i, 128)] = part[i, pl.ds(row + skip, depth), :]


def load_kernel(
    latent, momentum, counts_in, kappa_in, hyper, speed, size,
    state, inner, outer, low, table, raw, small, sems,
):
    field, moment, counts, kappa, _, _ = views(state)
    copies = [(hyper, small.at[pl.ds(0, 2)]), (speed, small.at[pl.ds(2, 2)])]
    copies.append((size, small.at[pl.ds(4, 1)]))
    for i in range(2):
        cols = pl.ds(128 * i, 128)
        own = pl.ds(TOP, SIZE)
        for c in range(2):
            copies.append((latent.at[c, :, cols], field.at[c, i, own, :]))
            copies.append((momentum.at[c, :, cols], moment.at[c, i, own, :]))
        copies.append((counts_in.at[:, cols], raw.at[i]))
        copies.append((kappa_in.at[:, cols], kappa.at[i, own, :]))
    copies = [pltpu.make_async_copy(a, b, sems.at[n]) for n, (a, b) in enumerate(copies)]
    for copy in copies:
        copy.start()
    for copy in copies:
        copy.wait()
    lane = lanes()
    parts = parts_of(state)

    def body(row, carry):
        here = pl.ds(row - TOP, 8)
        own = pl.ds(row, 8)
        for i in range(2):
            counts[i, own, :] = raw[i, here, :].astype(F32)
            kappa[i, own, :] += 4.0
        return carry

    loop(TOP, END, body, ())
    for c in range(2):
        for i in range(2):
            low[pl.ds(c, 1), pl.ds(128 * i, 128)] = field[c, i, pl.ds(TOP, 1), :]
    even = even_column()
    for row in range(0, HALF, 8):
        left, right = (pack_columns(parts, tile, row, lane) for tile in range(2))
        inner[pl.ds(row, 8), :] = jnp.where(even, right, left)
        outer[pl.ds(row, 8), :] = jnp.where(even, left, right)
    table[...] = jnp.zeros((8, 128), F32)
    table[pl.ds(0, 5), pl.ds(0, 2)] = small[...]


def local_sums_kernel(table, state, partial, up, down):
    field, _, counts, kappa, _, _ = views(state)
    lane = lanes()
    offset = table[pl.ds(OFFSET, 1), pl.ds(0, 2)]
    offsets = [splat(offset, c) for c in range(2)]

    def body(row, carry):
        carry = list(carry)
        inside = lax.broadcasted_iota(jnp.int32, (8, 128), 0) + row < END - 1
        for i in range(2):
            carry[4] += counts[i, pl.ds(row, 8), :]
        for c in range(2):
            tiles = [field[c, i, pl.ds(row, 8), :] for i in range(2)]
            right0 = pltpu.roll(tiles[0], 127, 1)
            right1 = pltpu.roll(tiles[1], 127, 1)
            beside = [jnp.where(lane == 127, right1, right0), jnp.where(lane == 127, 0.0, right1)]
            for i in range(2):
                below = jnp.where(inside, field[c, i, pl.ds(row + 1, 8), :], 0.0)
                weight = kappa[i, pl.ds(row, 8), :] * tiles[i]
                carry[c] += tiles[i] * (weight - 2.0 * (beside[i] + below))
                carry[2 + c] += jnp.exp(offsets[c] + tiles[i])
        return tuple(carry)

    put_sums(partial, loop(TOP, END, body, zeros(5)))
    pack_rows(up, parts_of(state), TOP, [0] * 6)
    pack_rows(down, parts_of(state), END - HALO, [HALO - depth for depth in DEPTHS])


def parts_of(state):
    field, moment, counts, kappa, _, _ = views(state)
    return [field.at[0], field.at[1], moment.at[0], moment.at[1], counts, kappa]


def unpack(from_right, from_left, lane, n, right_at, left_at):
    depth = DEPTHS[n]
    right = turned(from_right, -right_at - STARTS[n])
    left = turned(from_left, -depth - left_at - STARTS[n])
    return jnp.where(lane < depth, right, jnp.where(lane >= 128 - depth, left, 0.0))


def join_kernel(
    state_in, col_inner, col_outer, below, partial, up, down, state, spread, inner, outer
):
    del state_in
    even = even_column()
    lane = lanes()
    parts = parts_of(state)
    field = views(state)[0]
    edges = list(zeros(2))
    for half in range(2):
        for row in range(0, HALF, 8):
            a, b = col_inner[pl.ds(row, 8), :], col_outer[pl.ds(row, 8), :]
            right, left = jnp.where(even, a, b), jnp.where(even, b, a)
            own = pl.ds(TOP + HALF * half + row, 8)
            for n, part in enumerate(parts):
                tile = unpack(right, left, lane, n, 64 * half, 64 * half)
                part[2, own, :] = tile
                if n < 2:
                    edge = pltpu.roll(part[1, own, :], 1, 1) * tile
                    edges[n] += jnp.where(lane == 0, edge, 0.0)
    even_r = even_row()

    def put(rows, cols, high, low):
        inner[rows, cols] = jnp.where(even_r, low, high)
        outer[rows, cols] = jnp.where(even_r, high, low)

    for i in range(2):
        cols = pl.ds(128 * i, 128)
        for row in range(0, 64, 8):
            rows = pl.ds(row, 8)
            put(rows, cols, up[rows, cols], down[rows, cols])
        top, end = pl.ds(8 * i, 8), pl.ds(HALF - HALO + 8 * i, 8)
        (right, low_right), (left, low_left) = (
            [jnp.where(even, p[rows, :], q[rows, :]) for rows in (top, end)]
            for p, q in ((col_inner, col_outer), (col_outer, col_inner))
        )
        high = jnp.where(lane < 64, right, pltpu.roll(left, 64, 1))
        low = jnp.where(lane < 64, pltpu.roll(low_right, 64, 1), low_left)
        put(pl.ds(64, 8), cols, high, low)
    index = lax.broadcasted_iota(jnp.int32, (1, 128), 1)
    result = partial[pl.ds(0, 1), :]
    for c in range(2):
        total = jnp.sum(jnp.sum(edges[c], axis=0, keepdims=True), axis=1, keepdims=True)
        for i in range(2):
            own = field[c, i, pl.ds(END - 1, 1), :]
            other = below[pl.ds(c, 1), pl.ds(128 * i, 128)]
            total += jnp.sum(own * other, axis=1, keepdims=True)
        result -= jnp.where(index == c, 2.0 * total, 0.0)
    spread[...] = jnp.broadcast_to(result, spread.shape)


def unpack_rows(inner, outer, state):
    lane = lanes()
    parts = parts_of(state)
    even = even_row()

    def both(*at):
        a, b = inner[at], outer[at]
        return jnp.where(even, b, a), jnp.where(even, a, b)

    for n, (part, depth, start) in enumerate(zip(parts, DEPTHS, STARTS, strict=True)):
        for i in range(2):
            above, below = both(pl.ds(start, depth), pl.ds(128 * i, 128))
            part[i, pl.ds(TOP - depth, depth), :] = above
            part[i, pl.ds(END, depth), :] = below
    for i in range(2):
        above, below = both(pl.ds(64, 8), pl.ds(128 * i, 128))
        for n, part in enumerate(parts):
            part[2, pl.ds(GUARD + 8 * i, 8), :] = unpack(above, above, lane, n, 0, 64)
            part[2, pl.ds(END + 8 * i, 8), :] = unpack(below, below, lane, n, 0, 64)


def sum_of(received):
    return jnp.sum(received[...], axis=0, keepdims=True)


def read_table(table):
    return [table[pl.ds(i, 1), pl.ds(0, 2)] for i in range(6)]


def write_table(out, rows):
    out[...] = jnp.zeros((8, 128), F32)
    for i, row in enumerate(rows):
        out[pl.ds(i, 1), pl.ds(0, 2)] = row


def accel_of(quadratic, intensity, scale, count, total):
    return (intensity / total - count, 0.5 * jnp.exp(scale) * quadratic / total - 0.5)


def first_step_kernel(
    total, table, received, inner, outer, state_in, table_out, state, partial, other
):
    del state_in
    unpack_rows(inner, outer, state)
    field, moment, counts, kappa, slope, growth = views(state)
    reduced = sum_of(received)
    offset, scale, speed_0, speed_1, size, _ = read_table(table)
    quadratic, intensity = reduced[:, 0:2], reduced[:, 2:4]
    count = jnp.broadcast_to(reduced[:, 4:5], (1, 2)) / total
    a_0, a_1 = accel_of(quadratic, intensity, scale, count, total)
    advance(field, other, moment, counts, kappa, offset, jnp.exp(scale), size, 0.5, HALO)
    speed_0, speed_1 = speed_0 - 0.5 * size * a_0, speed_1 - 0.5 * size * a_1
    offset, scale = offset + size * speed_0, scale + size * speed_1
    near = advance(other, field, moment, counts, kappa, offset, jnp.exp(scale), size, 1.0, HALO)
    far = examine(field, kappa, slope, growth, offset - SHIFT, HALO // 2)
    put_sums(partial, (*near, *far))
    write_table(table_out, (offset, scale, speed_0, speed_1, size, count))


def two_params(table, received, total):
    reduced = sum_of(received)
    offset, scale, speed_0, speed_1, size, count = read_table(table)
    before = offset
    a_0, a_1 = accel_of(reduced[:, 0:2], reduced[:, 2:4], scale, count, total)
    speed_0, speed_1 = speed_0 - size * a_0, speed_1 - size * a_1
    offset, scale = offset + size * speed_0, scale + size * speed_1
    factor = jnp.exp(offset - before + SHIFT)
    intensity = reduced[:, 6:8] * factor
    a_0, a_1 = accel_of(reduced[:, 4:6], intensity, scale, count, total)
    return offset, scale, speed_0, speed_1, size, count, a_0, a_1, factor


def field_copies(field, out, sems, first):
    pairs = [(c, i) for c in ((0,) if first else (1,)) for i in range(2)]
    return [
        pltpu.make_async_copy(
            field.at[c, i, pl.ds(TOP, SIZE), :], out.at[c, :, pl.ds(128 * i, 128)], sems.at[n]
        )
        for n, (c, i) in enumerate(pairs)
    ]


def two_steps_kernel(
    total, final, table, received, state_in, table_out, state, partial, *more
):
    del state_in
    *latent_out, other = more[: 1 + final]
    field, moment, counts, kappa, slope, growth = views(state)
    offset, scale, speed_0, speed_1, size, count, a_0, a_1, factor = two_params(table, received, total)
    advance_known(
        field, other, moment, counts, slope, growth, factor, jnp.exp(scale), size, HALO // 2
    )
    speed_0, speed_1 = speed_0 - size * a_0, speed_1 - size * a_1
    offset, scale = offset + size * speed_0, scale + size * speed_1
    near = advance(other, field, moment, counts, kappa, offset, jnp.exp(scale), size, 1.0, HALO // 2)
    copies = []
    if final:
        copies = field_copies(field, latent_out[0], more[-1], True)
        for copy in copies:
            copy.start()
    far = examine(field, kappa, slope, growth, offset - SHIFT, HALO // 2)
    put_sums(partial, (*near, *far))
    write_table(table_out, (offset, scale, speed_0, speed_1, size, count))
    for copy in copies:
        copy.wait()


def last_kernel(
    total, table, received, state, latent_in,
    momentum_out, hyper_out, velocity_out, latent_out, result, small, sems, field_sems,
):
    del latent_in
    field_out = field_copies(views(state)[0], latent_out, field_sems, False)
    for copy in field_out:
        copy.start()
    _, moment, counts, _, slope, growth = views(state)
    offset, scale, speed_0, speed_1, size, _, a_0, a_1, factor = two_params(table, received, total)
    tau = jnp.exp(scale)
    taus = [splat(tau, c) for c in range(2)]
    factors = [splat(factor, c) for c in range(2)]
    halves = [0.5 * splat(size, c) for c in range(2)]
    for i, row in enumerate(
        (offset, scale, speed_0 - 0.5 * size * a_0, speed_1 - 0.5 * size * a_1)
    ):
        small[i // 2, pl.ds(i % 2, 1), :] = row
    copies = [
        pltpu.make_async_copy(small.at[0], hyper_out, sems.at[2 * PIECES]),
        pltpu.make_async_copy(small.at[1], velocity_out, sems.at[2 * PIECES + 1]),
    ]
    for copy in copies:
        copy.start()
    for n in range(PIECES):
        start = n * SIZE // PIECES
        rows = pl.ds(start, SIZE // PIECES)
        for row in range(TOP + start, TOP + start + SIZE // PIECES, 8):
            here = pl.ds(row, 8)
            for i in range(2):
                count = counts[i, here, :]
                for c in range(2):
                    gradient = taus[c] * slope[c, i, here, :] - count
                    gradient += factors[c] * growth[c, i, here, :]
                    value = moment[c, i, here, :] - halves[c] * gradient
                    result[c, pl.ds(row - TOP, 8), pl.ds(128 * i, 128)] = value
        for c in range(2):
            copies.append(
                pltpu.make_async_copy(
                    result.at[c, rows, :], momentum_out.at[c, rows, :], sems.at[2 * n + c]
                )
            )
            copies[-1].start()
    for copy in (*field_out, *copies):
        copy.wait()


def vmem(*shape):
    return pltpu.VMEM(shape, F32)


def held(array):
    return pltpu.with_memory_space_constraint(array, pltpu.VMEM)


STATE = vmem(10, 3, ROWS, 128)
PARAMS = pltpu.CompilerParams(vmem_limit_bytes=8 << 20)


def ring(x, axes, step):
    count = lax.axis_size(axes)
    return lax.ppermute(x, axes, [(i, (i + step) % count) for i in range(count)])


def swap(x, axes, first):
    count = lax.axis_size(axes)
    pairs = [((first + i) % count, (first + i + 1) % count) for i in range(0, count, 2)]
    return lax.ppermute(x, axes, [p for a, b in pairs for p in ((a, b), (b, a))])


def exchange(spread):
    shape = spread.shape
    spread = spread.reshape(shape[0], 1, shape[1])
    return lax.all_to_all(spread, ALL, 0, 0, tiled=True).reshape(shape)


def shards(latent, momentum, hyper_params, velocity, step_size, counts, kappa_field):
    devices = lax.axis_size(ALL)
    total = float(latent.shape[1] * latent.shape[2] * devices)
    spread = vmem(devices, 128)
    small_table = jax.ShapeDtypeStruct((8, 128), F32)
    given = (latent, momentum, counts, kappa_field, hyper_params, velocity, step_size[None])
    packed, strip = vmem(HALF, 128), vmem(STRIP, SIZE)
    state, inner, outer, low, table = pl.pallas_call(
        load_kernel,
        out_shape=(STATE, packed, packed, vmem(2, SIZE), vmem(8, 128)),
        in_specs=[ANY] * 7,
        out_specs=(VMEM,) * 5,
        scratch_shapes=[
            pltpu.VMEM((2, SIZE, 128), jnp.int32),
            vmem(5, 2),
            pltpu.SemaphoreType.DMA((15,)),
        ],
        compiler_params=PARAMS,
        name="load",
    )(*(pltpu.with_memory_space_constraint(a, pltpu.HBM) for a in given))
    below = ring(low, ROW, -1)
    inner, outer = swap(inner, COL, 0), swap(outer, COL, 1)
    partial, up, down = pl.pallas_call(
        local_sums_kernel,
        out_shape=(vmem(8, 128), strip, strip),
        in_specs=[VMEM] * 2,
        out_specs=(VMEM,) * 3,
        compiler_params=PARAMS,
        name="local_sums",
    )(held(table), held(state))
    state, partial, row_inner, row_outer = pl.pallas_call(
        join_kernel,
        out_shape=(STATE, spread, strip, strip),
        in_specs=[VMEM] * 7,
        out_specs=(VMEM,) * 4,
        input_output_aliases={0: 0},
        compiler_params=PARAMS,
        name="join",
    )(held(state), inner, outer, below, partial, held(up), held(down))
    row_inner, row_outer = swap(row_inner, ROW, 0), swap(row_outer, ROW, 1)
    received = exchange(partial)
    table, state, partial = pl.pallas_call(
        functools.partial(first_step_kernel, total),
        out_shape=(small_table, STATE, spread),
        in_specs=[VMEM] * 5,
        out_specs=(VMEM,) * 3,
        input_output_aliases={4: 1},
        scratch_shapes=[vmem(2, 3, ROWS, 128)],
        compiler_params=PARAMS,
        name="first_steps",
    )(table, received, row_inner, row_outer, held(state))
    latent_out = ()
    result = jax.ShapeDtypeStruct(latent.shape, F32)
    for index in range(STEPS // 2 - 1):
        received = exchange(partial)
        final = index == STEPS // 2 - 2
        table, state, partial, *latent_out = pl.pallas_call(
            functools.partial(two_steps_kernel, total, final),
            out_shape=(small_table, STATE, spread) + final * (result,),
            in_specs=[VMEM] * 3,
            out_specs=(VMEM,) * 3 + final * (ANY,),
            input_output_aliases={2: 1},
            scratch_shapes=[vmem(2, 3, ROWS, 128)] + final * [pltpu.SemaphoreType.DMA((2,))],
            compiler_params=PARAMS,
            name="two_steps",
        )(table, received, held(state))
    received = exchange(partial)
    momentum_out, hyper_out, velocity_out, latent_out = pl.pallas_call(
        functools.partial(last_kernel, total),
        out_shape=(
            result,
            jax.ShapeDtypeStruct((2, 2), F32),
            jax.ShapeDtypeStruct((2, 2), F32),
            result,
        ),
        in_specs=[VMEM] * 3 + [ANY],
        out_specs=(ANY,) * 4,
        input_output_aliases={3: 3},
        scratch_shapes=[
            vmem(*latent.shape),
            vmem(2, 2, 2),
            pltpu.SemaphoreType.DMA((2 * PIECES + 2,)),
            pltpu.SemaphoreType.DMA((2,)),
        ],
        compiler_params=PARAMS,
        name="last",
    )(table, received, held(state), latent_out[0])
    return latent_out, momentum_out, hyper_out, velocity_out


def solution(mesh):
    torus = Mesh(mesh.devices.reshape(2, 4, 2, 4, 2), ALL)
    return jax.shard_map(
        shards,
        mesh=torus,
        in_specs=(P(None, ROW, COL), P(None, ROW, COL), P(), P(), P(), P(ROW, COL), P(ROW, COL)),
        out_specs=(P(None, ROW, COL), P(None, ROW, COL), P(), P()),
        check_vma=False,
    )
```
